256 devices in a mesh: req: 8 (over y, core), tp: 32 (over z, x).
Axes of the slice: x: 4, y: 4, z: 8, core: 2. Of those that a mesh axis runs over, the one named last changes fastest.
Arguments:
- queries: bfloat16 [1024, 1536], P(('req', 'tp')), may hold values from -8 to 8
- new_kv: bfloat16 [1024, 1024], P(('req', 'tp')), may hold values from -6 to 6
- residual: bfloat16 [1024, 1536], P(('req', 'tp')), may hold values from -6 to 6
- placement: int32 [16], P('req'), may hold values from 0 to 15, as said below
- lengths: int32 [16], P('req'), may hold values from 2 to 4096
- page_table: int32 [16, 1, 32], P('req', None, 'tp'), may hold values from 0 to 1, as said below
- cache_keys: bfloat16 [512, 128, 512], P(('req', 'tp')), may hold values from -6 to 6
- cache_values: bfloat16 [512, 128, 512], P(('req', 'tp')), may hold values from -6 to 6
- parents: int32 [16, 64], P('req'), may hold values from 0 to 62, as said below
- accept_leaf: int32 [16], P('req'), may hold values from 0 to 63
- out_weight: bfloat16 [1536, 1536], replicated, may hold values from -0.15625 to 0.15625
- norm_gain: float32 [1536], replicated, may hold values from 0.1 to 1.9
- router_weight: bfloat16 [1536, 40], replicated, may hold values from -0.15625 to 0.15625
- expert_ids: int32 [1024, 8], P('req'), may hold values from 0 to 39, all different within a row
- gate_up: bfloat16 [160, 1536, 256], P('tp'), may hold values from -0.15625 to 0.15625
- down_weight: bfloat16 [160, 128, 1536], P('tp'), may hold values from -0.25 to 0.25
Outputs:
- attn_out: bfloat16 [1024, 1536], P(('req', 'tp'))
- layer_out: bfloat16 [1024, 1536], P(('req', 'tp'))
- accepted_kv: bfloat16 [1024, 1024], P(('req', 'tp'))
The draws below stay inside these ranges and needn't reach their ends.
Inputs may be any that keep to these rules, and one draw needn't show every extreme that they name: `placement`: slot s of each group of 2 slots holds a request whose index is s modulo 2; every request is held once. `page_table`: within each group of 2 slots and each last index, the 2 entries are distinct. parents[s, n] < n for n > 0; parents[s, 0] = 0.
All inputs are finite; a program needn't handle non-finite values.
Results may differ from the reference program's by a relative error of at most 0.01.
Values may be sent and summed in bfloat16 or wider, within the bound.
A program may use at most 128 MiB of HBM per device.

```python
import math
import jax
import jax.numpy as jnp
from jax import lax

D = 1536
HEADS = 24
KV_HEADS = 8
HEAD = 64
EXPERTS = 40
FF_E = 512
TOPK = 8
UNIT = 128
DRAFT = 64
PAGE = 128
LOCAL_PAGES = 1
REQ_DEV = 2
REQS = 16
TOKENS = 1024
UNITS = 160
MAXPAGES = 32
MAXLEN = 4096
PAGES = 512
N_TP = 32


def draw_queries(key, part):
    fresh_key = jax.random.fold_in(key, 11)
    base_draw = jnp.clip(2.0 * jax.random.normal(fresh_key, (TOKENS, HEADS, HEAD), jnp.float32), -8.0, 8.0)
    return base_draw.reshape(TOKENS, HEADS * HEAD).astype(jnp.bfloat16)


def draw_cache_keys(key, part):
    fresh_key = jax.random.fold_in(key, 23)
    base_draw = jnp.clip(jax.random.normal(fresh_key, (PAGES, PAGE, KV_HEADS, HEAD), jnp.float32), -6.0, 6.0)
    return base_draw.reshape(PAGES, PAGE, KV_HEADS * HEAD).astype(jnp.bfloat16)


def permute_groups(one_key):
    return jax.random.permutation(one_key, REQS // REQ_DEV)


def draw_placement(key, part):
    slot_keys = jax.random.split(jax.random.fold_in(key, 31), REQ_DEV)
    orders = jax.vmap(permute_groups)(slot_keys)
    slot_ids = jnp.arange(REQ_DEV, dtype=jnp.int32)
    placed = jnp.transpose(orders).astype(jnp.int32) * REQ_DEV + slot_ids[None, :]
    return placed.reshape(REQS).astype(jnp.int32)


def draw_lengths(key, part):
    base_draw = jax.random.randint(jax.random.fold_in(key, 41), (REQS,), 2, MAXLEN + 1)
    shifts = jax.random.randint(jax.random.fold_in(key, 43), (REQS,), 0, 6)
    drawn = jnp.maximum(jnp.right_shift(base_draw, shifts), 2)
    top_index = jax.random.randint(jax.random.fold_in(key, 45), (), 0, REQS // 2)
    low_index = REQS // 2 + jax.random.randint(jax.random.fold_in(key, 47), (), 0, REQS - REQS // 2)
    drawn = drawn.at[top_index].set(MAXLEN)
    drawn = drawn.at[low_index].set(2)
    return drawn.astype(jnp.int32)


def permute_pool(one_key):
    return jax.random.permutation(one_key, REQ_DEV * LOCAL_PAGES)


def draw_page_table(key, part):
    columns = PAGES // (REQS * LOCAL_PAGES)
    group_count = REQS // REQ_DEV
    pool_keys = jax.random.split(jax.random.fold_in(key, 53), group_count * columns)
    orders = jax.vmap(permute_pool)(pool_keys)
    table = orders.reshape(group_count, columns, REQ_DEV, LOCAL_PAGES)
    return jnp.transpose(table, (0, 2, 3, 1)).reshape(REQS, LOCAL_PAGES, columns).astype(jnp.int32)


def draw_parents(key, part):
    node_ids = jnp.arange(DRAFT, dtype=jnp.int32)
    raw_draw = jax.random.randint(jax.random.fold_in(key, 61), (REQS, DRAFT), 0, 1 << 20)
    drawn = raw_draw % jnp.maximum(node_ids, 1)[None, :]
    drawn = drawn.at[:, DRAFT - 1].set(DRAFT - 2)
    return drawn.astype(jnp.int32)


def draw_accept_leaf(key, part):
    drawn = jax.random.randint(jax.random.fold_in(key, 71), (REQS,), 0, DRAFT)
    top_index = jax.random.randint(jax.random.fold_in(key, 73), (), 0, REQS // 2)
    low_index = REQS // 2 + jax.random.randint(jax.random.fold_in(key, 75), (), 0, REQS - REQS // 2)
    drawn = drawn.at[top_index].set(DRAFT - 1)
    drawn = drawn.at[low_index].set(0)
    return drawn.astype(jnp.int32)


def shard_levels(own_key, dims, pieces, low, top_value):
    factor_of = 1.0
    for position, shards_of in pieces:
        draws = jax.random.uniform(jax.random.fold_in(jax.random.fold_in(own_key, 6), position), (shards_of,), jnp.float32, low / len(pieces), top_value / len(pieces))
        factor_of = factor_of * jnp.repeat(jnp.exp(draws), dims[position] // shards_of).reshape((-1,) + (1,) * (len(dims) - 1 - position))
    return factor_of


def distinct(rng, rows, count, top, lift):
    order = jax.random.permutation(jax.random.fold_in(rng, 1), count)
    pull = order
    for power in range(3):
        pull = pull * pull // count
    pull = pull * lift // count
    tickets = jax.random.randint(jax.random.fold_in(rng, 2), (rows, count), 0, 4096) + pull
    fixed_rows = jax.random.permutation(jax.random.fold_in(rng, 3), rows)[jnp.arange(count) % rows]
    tickets = jnp.where(jnp.arange(rows)[:, None] == fixed_rows[None, :], 1 << 14, tickets)
    score = tickets * count + jnp.arange(count)
    return lax.top_k(score.astype(jnp.int32), top)[1].astype(jnp.int32)


def bell_draw(own_key, shape, deviation, bound, pieces=(), kind=jnp.bfloat16):
    array = deviation * jax.random.normal(own_key, shape, jnp.float32)
    if pieces:
        array = array * shard_levels(own_key, shape, pieces, -0.22, 0.18)
    return jnp.clip(array, -bound, bound).astype(kind)


def setup_inputs(seed: int = 0) -> dict:
    key_list = jax.random.split(jax.random.key(seed), 17)
    return {
        "queries": draw_queries(jax.random.fold_in(key_list[16], 71), 0),
        "new_kv": bell_draw(key_list[1], (TOKENS, 2 * KV_HEADS * HEAD), 1.0, 6.0, ((0, 256),)),
        "residual": bell_draw(key_list[2], (TOKENS, D), 1.0, 6.0, ((0, 256),)),
        "placement": draw_placement(jax.random.fold_in(key_list[16], 71), 0),
        "lengths": draw_lengths(jax.random.fold_in(key_list[16], 71), 0),
        "page_table": draw_page_table(jax.random.fold_in(key_list[16], 71), 0),
        "cache_keys": draw_cache_keys(jax.random.fold_in(key_list[16], 71), 0),
        "cache_values": bell_draw(key_list[7], (PAGES, PAGE, KV_HEADS * HEAD), 1.0, 6.0, ((0, 256),)),
        "parents": draw_parents(jax.random.fold_in(key_list[16], 71), 0),
        "accept_leaf": draw_accept_leaf(jax.random.fold_in(key_list[16], 71), 0),
        "out_weight": bell_draw(key_list[10], (HEADS * HEAD, D), (HEADS * HEAD) ** -0.5, 0.15625),
        "norm_gain": jnp.clip(1.0 + 0.18 * jax.random.normal(key_list[11], (D,), jnp.float32), 0.1, 1.9),
        "router_weight": bell_draw(key_list[12], (D, EXPERTS), D ** -0.5, 0.15625),
        "expert_ids": distinct(key_list[13], TOKENS, EXPERTS, TOPK, 3276),
        "gate_up": bell_draw(key_list[14], (UNITS, D, 2 * UNIT), D ** -0.5, 0.15625, ((0, 32),)),
        "down_weight": bell_draw(key_list[15], (UNITS, UNIT, D), FF_E ** -0.5, 0.25, ((0, 32),)),
    }


neg_big = -1e+30
norm_eps = 1e-06

def ancestry(parents):
    node_count = parents.shape[-1]
    node_ids = jnp.arange(node_count, dtype=jnp.int32)
    linked = (parents[:, :, None] == node_ids[None, None, :]) & (node_ids[None, :, None] > 0)
    reached = jnp.maximum(linked.astype(jnp.float32), jnp.eye(node_count, dtype=jnp.float32)[None])
    for _ in range(node_count.bit_length()):
        reached = jnp.minimum(jnp.einsum('rnm,rmk->rnk', reached, reached, precision=lax.Precision.HIGHEST), 1.0)
    return reached

def reference(queries, new_kv, residual, placement, lengths, page_table, cache_keys, cache_values, parents, accept_leaf, out_weight, norm_gain, router_weight, expert_ids, gate_up, down_weight):
    group_size = HEADS // KV_HEADS
    kv_width = KV_HEADS * HEAD
    score_scale = 1.0 / math.sqrt(HEAD)
    pool_size = REQ_DEV * LOCAL_PAGES
    placed_q = jnp.take(queries.reshape(REQS, DRAFT, HEADS * HEAD), placement, axis=0)
    placed_kv = jnp.take(new_kv.reshape(REQS, DRAFT, 2 * kv_width), placement, axis=0)
    placed_res = jnp.take(residual.reshape(REQS, DRAFT, D), placement, axis=0).reshape(TOKENS, D)
    reached = ancestry(parents)
    page_index = jnp.arange(MAXPAGES, dtype=jnp.int32)
    page_col = page_index % N_TP
    page_loc = page_index // N_TP
    slot_index = jnp.arange(REQS, dtype=jnp.int32)
    node_ids = jnp.arange(DRAFT, dtype=jnp.int32)

    def one_slot(slot_items):
        slot_id, q_rows, kv_rows, slot_len, table_row, reach_slot, leaf_node = slot_items
        page_ids = (slot_id // REQ_DEV * N_TP + page_col) * pool_size + table_row[page_loc, page_col]
        keys_slot = jnp.take(cache_keys, page_ids, axis=0).reshape(MAXPAGES, PAGE, KV_HEADS, HEAD).astype(jnp.float32)
        values_slot = jnp.take(cache_values, page_ids, axis=0).reshape(MAXPAGES, PAGE, KV_HEADS, HEAD).astype(jnp.float32)
        query_blocks = q_rows.astype(jnp.float32).reshape(DRAFT, KV_HEADS, group_size, HEAD)
        scores = jnp.einsum('sgrd,ptgd->sgrpt', query_blocks, keys_slot) * score_scale
        positions = page_index[:, None] * PAGE + jnp.arange(PAGE, dtype=jnp.int32)[None, :]
        is_valid = (positions < slot_len)[None, None, None]
        scores = jnp.where(is_valid, scores, neg_big)
        block_max = lax.optimization_barrier(jnp.max(scores, axis=-1))
        weights = jnp.where(is_valid, jnp.exp(scores - block_max[..., None]), 0.0).astype(jnp.bfloat16).astype(jnp.float32)
        block_sum = lax.optimization_barrier(jnp.sum(weights, axis=-1))
        block_out = jnp.einsum('sgrpt,ptgd->sgrpd', weights, values_slot)
        tree_keys = kv_rows[:, :kv_width].astype(jnp.float32).reshape(DRAFT, KV_HEADS, HEAD)
        tree_values = kv_rows[:, kv_width:].astype(jnp.float32).reshape(DRAFT, KV_HEADS, HEAD)
        tree_scores = jnp.einsum('sgrd,tgd->sgrt', query_blocks, tree_keys) * score_scale
        tree_mask = (reach_slot > 0.5)[:, None, None, :]
        tree_scores = jnp.where(tree_mask, tree_scores, neg_big)
        tree_max = lax.optimization_barrier(jnp.max(tree_scores, axis=-1))
        tree_weights = jnp.where(tree_mask, jnp.exp(tree_scores - tree_max[..., None]), 0.0).astype(jnp.bfloat16).astype(jnp.float32)
        tree_sum = lax.optimization_barrier(jnp.sum(tree_weights, axis=-1))
        tree_out = jnp.einsum('sgrt,tgd->sgrd', tree_weights, tree_values)
        top_score = jnp.maximum(lax.optimization_barrier(jnp.max(block_max, axis=-1)), tree_max)
        block_scale = jnp.exp(block_max - top_score[..., None])
        tree_scale = jnp.exp(tree_max - top_score)
        running = lax.optimization_barrier(jnp.sum(block_sum * block_scale, axis=-1)) + tree_sum * tree_scale
        summed = jnp.einsum('sgrp,sgrpd->sgrd', block_scale, block_out) + tree_out * tree_scale[..., None]
        attn_rows = (summed / running[..., None]).reshape(DRAFT, HEADS * HEAD).astype(jnp.bfloat16)
        path_flags = (jnp.take(reach_slot, leaf_node, axis=0) > 0.5).astype(jnp.int32)
        path_rank = jnp.cumsum(path_flags) - 1
        select = ((path_flags[None, :] > 0) & (path_rank[None, :] == node_ids[:, None])).astype(jnp.float32)
        accepted_rows = jnp.dot(select, kv_rows.astype(jnp.float32), precision=lax.Precision.HIGHEST).astype(jnp.bfloat16)
        return (attn_rows, accepted_rows)
    attn_all, accepted_all = lax.map(one_slot, (slot_index, placed_q, placed_kv, lengths, page_table, reached, accept_leaf))
    attn_out = attn_all.reshape(TOKENS, HEADS * HEAD)
    hidden = placed_res.astype(jnp.float32) + jnp.dot(attn_out, out_weight, preferred_element_type=jnp.float32)
    normed = (hidden * lax.rsqrt(lax.optimization_barrier(jnp.mean(hidden * hidden, axis=-1, keepdims=True)) + norm_eps) * norm_gain.astype(jnp.float32)).astype(jnp.bfloat16)
    logits = jnp.dot(normed, router_weight, preferred_element_type=jnp.float32)
    onehot = (expert_ids[:, :, None] == jnp.arange(EXPERTS, dtype=jnp.int32)[None, None, :]).astype(jnp.float32)
    chosen = lax.optimization_barrier(jnp.sum(logits[:, None, :] * onehot, axis=-1))
    expo_chosen = jnp.exp(chosen)
    expert_probs = expo_chosen / lax.optimization_barrier(jnp.sum(expo_chosen, axis=-1, keepdims=True))
    routing = lax.optimization_barrier(jnp.sum(expert_probs[:, :, None] * onehot, axis=1))
    unit_span = FF_E // UNIT

    def add_unit(running, unit_items):
        unit_id, weights_gu, weights_down = unit_items
        gate_both = jnp.dot(normed, weights_gu, preferred_element_type=jnp.float32)
        share = lax.dynamic_slice_in_dim(routing, (unit_id // unit_span).astype(jnp.int32), 1, 1)
        activated = (jax.nn.silu(gate_both[:, :UNIT]) * gate_both[:, UNIT:] * share).astype(jnp.bfloat16)
        return (running + jnp.dot(activated, weights_down, preferred_element_type=jnp.float32), None)
    moe, _ = lax.scan(add_unit, jnp.zeros((TOKENS, D), jnp.float32), (jnp.arange(UNITS, dtype=jnp.int32), gate_up, down_weight))
    layer_out = (hidden + moe).astype(jnp.bfloat16)
    return (attn_out, layer_out, accepted_all.reshape(TOKENS, 2 * kv_width))
```

```python
import jax
import jax.numpy as jnp
from jax import lax
from jax.experimental import pallas as pl
from jax.experimental.pallas import tpu as pltpu
from jax.sharding import PartitionSpec as P

HEADS = 24
KV_HEADS = 8
HEAD = 64
D = 1536
EXPERTS = 40
FF_E = 512
UNIT = 128
UNITS_DEV = 5
DRAFT = 64
PAGE = 128
N_REQ = 8
N_TP = 32
TOK = 4
CHUNKS = 4
CW = D // CHUNKS
HALF = N_TP // 2
ROWS = CHUNKS * TOK
GROUP = N_TP * TOK

neg_big = -1e30
norm_eps = 1e-06
MESH = pl.DeviceIdType.MESH
f32 = jnp.float32
bf16 = jnp.bfloat16


def iota(shape, dim):
    return lax.broadcasted_iota(jnp.int32, shape, dim)


def ones_at(mask):
    return jnp.where(mask, 1.0, 0.0).astype(bf16)


def dot(a, b):
    return jnp.dot(a, b, preferred_element_type=f32)


def dot_t(a, b):
    return lax.dot_general(a, b, (((1,), (1,)), ((), ())), preferred_element_type=f32)


def softmax_block(stacked, keys, values, lo, hi, ones_rhs, valid):
    count = keys.shape[0]
    keys_two = jnp.concatenate([keys * lo, keys * hi], axis=0)
    values_two = jnp.concatenate([values * lo, values * hi], axis=0)
    scores = dot_t(stacked, keys_two)
    s_lo = jnp.where(valid, scores[:, :count], neg_big)
    s_hi = jnp.where(valid, scores[:, count:], neg_big)
    m_lo = jnp.max(s_lo, axis=1, keepdims=True)
    m_hi = jnp.max(s_hi, axis=1, keepdims=True)
    w_lo = jnp.where(valid, jnp.exp(s_lo - m_lo), 0.0).astype(bf16)
    w_hi = jnp.where(valid, jnp.exp(s_hi - m_hi), 0.0).astype(bf16)
    weights = jnp.concatenate([w_lo, w_hi], axis=1)
    both = dot(weights, jnp.concatenate([values_two, ones_rhs], axis=1))
    out, total = both[:, :128], both[:, 128:]
    rows = out.shape[0]
    first = iota((rows, 128), 1) < HEAD
    top = jnp.where(first, m_lo, m_hi)
    some = total > 0.0
    safe = jnp.where(some, total, 1.0)
    return out / safe, jnp.where(some, top + jnp.log(safe), neg_big)


def two_ones(count):
    row = iota((2 * count, 128), 0)
    lane = iota((2 * count, 128), 1)
    return ones_at((row >= count) == (lane >= HEAD))


def kernel(
    placement, lengths, table, leaf,
    q_ref, kv_ref, res_ref, par_ref, gain_ref, ids_ref,
    keys_hbm, vals_hbm, ow_hbm, rw_hbm, gu_hbm, dw_hbm,
    attn_ref, layer_ref, acc_ref,
    kbuf, vbuf, ow, rw, gu, dw,
    q8, r8, qall, kvall, osend, orecv, nall, msend, mrecv,
    chunk_s, flat_s, res_s, perm_s, permt_s, outs_s, nfull, act_s, moe_s,
    wsem, s_q8, r_q8, s_r8, r_r8, s_q, r_q, s_kv, r_kv, s_o, r_o, s_n, r_n, s_m, r_m,
):
    g = lax.axis_index("req")
    t = lax.axis_index("tp")
    half = t // HALF
    t_in = t % HALF

    def req_peer(k):
        return lax.rem(g + k, N_REQ)

    def tp_peer(k):
        return lax.rem(t // 4 + k // 4, 8) * 4 + lax.rem(t % 4 + k % 4, 4)

    def slot_peer(k):
        return half * HALF + lax.rem(t_in + k, HALF)

    barrier = pltpu.get_barrier_semaphore()

    def greet_req(k, carry):
        pl.semaphore_signal(barrier, inc=1, device_id={"req": req_peer(k)}, device_id_type=MESH)
        return carry

    def greet_tp(k, carry):
        pl.semaphore_signal(barrier, inc=1, device_id={"tp": tp_peer(k)}, device_id_type=MESH)
        return carry

    lax.fori_loop(1, N_REQ, greet_req, 0)
    lax.fori_loop(1, N_TP, greet_tp, 0)

    loads = [
        pltpu.make_async_copy(a, b, wsem.at[i])
        for i, (a, b) in enumerate(
            [(keys_hbm, kbuf), (vals_hbm, vbuf), (ow_hbm, ow), (rw_hbm, rw), (gu_hbm, gu), (dw_hbm, dw)]
        )
    ]
    for load in loads:
        load.start()

    q_in = q_ref[...].astype(f32) * (HEAD ** -0.5)
    for c in range(CHUNKS):
        for r in range(3):
            for k in range(2):
                at = c * CW + (k * 3 + r) * HEAD
                chunk_s[c * TOK:(c + 1) * TOK, (2 * r + k) * HEAD:(2 * r + k + 1) * HEAD] = (
                    q_in[:, at:at + HEAD]
                )
    q8[g] = chunk_s[...].astype(bf16)
    kv_in = kv_ref[...].astype(f32)
    for c in range(CHUNKS):
        chunk_s[c * TOK:(c + 1) * TOK, 0:128] = kv_in[:, c * 128:(c + 1) * 128]
        chunk_s[c * TOK:(c + 1) * TOK, 128:256] = kv_in[:, 512 + c * 128:512 + (c + 1) * 128]
    r8[g, :, 0:256] = chunk_s[:, 0:256].astype(bf16)
    res_in = res_ref[...].astype(f32)
    for c in range(CHUNKS):
        chunk_s[c * TOK:(c + 1) * TOK, :] = res_in[:, c * CW:(c + 1) * CW]
    r8[g, :, 256:640] = chunk_s[...].astype(bf16)

    def q8_copy(k, source):
        return pltpu.make_async_remote_copy(
            src_ref=q8.at[source], dst_ref=q8.at[source], send_sem=s_q8.at[k],
            recv_sem=r_q8.at[source], device_id={"req": req_peer(k)}, device_id_type=MESH,
        )

    def r8_copy(k, source):
        return pltpu.make_async_remote_copy(
            src_ref=r8.at[source], dst_ref=r8.at[source], send_sem=s_r8.at[k],
            recv_sem=r_r8.at[source], device_id={"req": req_peer(k)}, device_id_type=MESH,
        )

    def q_copy(k, source):
        return pltpu.make_async_remote_copy(
            src_ref=qall.at[source], dst_ref=qall.at[source], send_sem=s_q.at[k],
            recv_sem=r_q.at[source], device_id={"tp": tp_peer(k)}, device_id_type=MESH,
        )

    def kv_copy(k, source):
        return pltpu.make_async_remote_copy(
            src_ref=kvall.at[source], dst_ref=kvall.at[source], send_sem=s_kv.at[k],
            recv_sem=r_kv.at[source], device_id={"tp": slot_peer(k)}, device_id_type=MESH,
        )

    def o_copy(k, block, source):
        return pltpu.make_async_remote_copy(
            src_ref=osend.at[block], dst_ref=orecv.at[source], send_sem=s_o.at[k],
            recv_sem=r_o.at[source], device_id={"tp": tp_peer(k)}, device_id_type=MESH,
        )

    def n_copy(k, source):
        return pltpu.make_async_remote_copy(
            src_ref=nall.at[source], dst_ref=nall.at[source], send_sem=s_n.at[k],
            recv_sem=r_n.at[source], device_id={"tp": tp_peer(k)}, device_id_type=MESH,
        )

    def m_copy(k, block, source):
        return pltpu.make_async_remote_copy(
            src_ref=msend.at[block], dst_ref=mrecv.at[source], send_sem=s_m.at[k],
            recv_sem=r_m.at[source], device_id={"tp": tp_peer(k)}, device_id_type=MESH,
        )

    def each(count, step):
        def body(k, carry):
            step(k)
            return carry

        lax.fori_loop(1, count, body, 0)

    row_a = iota((256, 256), 0)
    row_b = iota((256, 256), 1)
    perm_s[...] = ones_at(
        row_b == ((row_a & 63) >> 2) * ROWS + (row_a >> 6) * TOK + (row_a & 3)
    )
    permt_s[...] = ones_at(
        row_a == ((row_b & 63) >> 2) * ROWS + (row_b >> 6) * TOK + (row_b & 3)
    )

    pl.semaphore_wait(barrier, N_REQ - 1 + N_TP - 1)

    each(N_REQ, lambda k: q8_copy(k, g).start())
    each(N_REQ, lambda k: r8_copy(k, g).start())

    node_m = iota((DRAFT, DRAFT), 0)
    node_n = iota((DRAFT, DRAFT), 1)
    parent_row = par_ref[pl.ds(half, 1), :]
    reach_t = ones_at(((node_m == parent_row) & (node_n > 0)) | (node_m == node_n))
    for _ in range(6):
        reach_t = jnp.minimum(dot(reach_t, reach_t), 1.0).astype(bf16)
    own_node = t_in * TOK + (iota((ROWS, DRAFT), 0) & 3)
    lane_node = iota((ROWS, DRAFT), 1)
    spread_row = iota((DRAFT, 256), 0)
    spread_lane = iota((DRAFT, 256), 1)
    spread = ones_at(spread_row == (spread_lane >> 4) * TOK + (spread_lane & 3))
    same_chunk = ((iota((ROWS, 256), 1) >> 2) & 3) == (iota((ROWS, 256), 0) >> 2)
    own_reach = dot_t(ones_at(lane_node == own_node), reach_t).astype(bf16)
    tree_mask = jnp.where(same_chunk, dot(own_reach, spread), 0.0)
    flags = dot_t(ones_at(lane_node == leaf[half]), reach_t)
    rank = dot(flags.astype(bf16), ones_at(node_m <= node_n)) - 1.0
    chosen = ones_at((flags > 0.5) & (rank == own_node.astype(f32)))
    choice = jnp.where(same_chunk, dot(chosen, spread), 0.0).astype(bf16)

    lane_one = iota((1, 128), 1)
    lo = ones_at(lane_one < HEAD)
    hi = ones_at(lane_one >= HEAD)

    each(N_REQ, lambda k: q8_copy(k, req_peer(k)).wait_recv())
    source_group = lax.shift_right_logical(placement[half], 1)
    own_q = q8[source_group]
    qall[t] = own_q
    each(N_TP, lambda k: q_copy(k, t).start())
    each(N_REQ, lambda k: r8_copy(k, req_peer(k)).wait_recv())
    own_kvres = r8[source_group]
    kvall[t_in] = own_kvres[:, 0:256]
    each(HALF, lambda k: kv_copy(k, t_in).start())
    own_res = own_kvres[:, 256:640].astype(f32)
    for c in range(CHUNKS):
        res_s[0:TOK, c * CW:(c + 1) * CW] = own_res[c * TOK:(c + 1) * TOK, :]

    ones_page = two_ones(PAGE)
    loads[0].wait()
    loads[1].wait()
    each(N_TP, lambda k: q_copy(k, tp_peer(k)).wait_recv())
    stat_lane = iota((DRAFT, 128), 1)
    piece = stat_lane & 7
    stat_r = (stat_lane & 63) >> 3
    for s in range(2):
        q_slot = dot(perm_s[...], qall[s * HALF:(s + 1) * HALF].reshape(256, CW)).astype(bf16)
        page = table[s]
        page_k = kbuf[page]
        page_v = vbuf[page]
        valid = t * PAGE + iota((1, PAGE), 1) < lengths[s]
        for c in range(CHUNKS):
            q_c = q_slot[c * DRAFT:(c + 1) * DRAFT]
            stacked = jnp.concatenate([q_c[:, r * 128:(r + 1) * 128] for r in range(3)], axis=0)
            out, lse = softmax_block(
                stacked, page_k[:, c * 128:(c + 1) * 128], page_v[:, c * 128:(c + 1) * 128],
                lo, hi, ones_page, valid,
            )
            stats = jnp.zeros((DRAFT, 128), f32)
            for r in range(3):
                outs_s[c * DRAFT:(c + 1) * DRAFT, r * 128:(r + 1) * 128] = (
                    out[r * DRAFT:(r + 1) * DRAFT].astype(bf16)
                )
                part = lse[r * DRAFT:(r + 1) * DRAFT]
                first = part.astype(bf16).astype(f32)
                rest = part - first
                second = rest.astype(bf16).astype(f32)
                third = rest - second
                value = jnp.where(piece == 0, first, jnp.where(piece == 1, second, third))
                stats = jnp.where((stat_r == r) & (piece < 3), value, stats)
            outs_s[c * DRAFT:(c + 1) * DRAFT, CW:512] = stats.astype(bf16)
        osend[s * HALF:(s + 1) * HALF] = (
            dot(permt_s[...], outs_s[...]).astype(bf16).reshape(HALF, ROWS, 512)
        )

    each(N_TP, lambda k: o_copy(k, tp_peer(k), t).start())
    orecv[t] = osend[t]

    each(HALF, lambda k: kv_copy(k, lax.rem(t_in + k, HALF)).wait_recv())
    kv_slot = kvall[...].reshape(256, 256)
    accepted = dot(choice, kv_slot)
    for c in range(CHUNKS):
        acc_ref[:, c * 128:(c + 1) * 128] = accepted[c * TOK:(c + 1) * TOK, 0:128].astype(bf16)
        acc_ref[:, 512 + c * 128:512 + (c + 1) * 128] = (
            accepted[c * TOK:(c + 1) * TOK, 128:256].astype(bf16)
        )
    q_own = jnp.concatenate([own_q[:, r * 128:(r + 1) * 128] for r in range(3)], axis=0)
    tree_valid = jnp.concatenate([tree_mask] * 3, axis=0) > 0.5
    tree_out, tree_lse = softmax_block(
        q_own, kv_slot[:, 0:128], kv_slot[:, 128:256], lo, hi, two_ones(256), tree_valid
    )
    tree_out = jnp.concatenate([tree_out[r * ROWS:(r + 1) * ROWS] for r in range(3)], axis=1)
    tree_lse = jnp.concatenate([tree_lse[r * ROWS:(r + 1) * ROWS] for r in range(3)], axis=1)
    ex_l = iota((128, CW), 0)
    ex_c = iota((128, CW), 1)
    expand = ones_at(
        ((ex_l >> 6) == ((ex_c >> 6) & 1)) & (((ex_l & 63) >> 3) == (ex_c >> 7)) & ((ex_l & 7) < 3)
    )

    each(N_TP, lambda k: o_copy(k, 0, tp_peer(k)).wait_recv())
    lse_all = dot(orecv[:, :, CW:512].reshape(N_TP * ROWS, 128), expand).reshape(N_TP, ROWS, CW)
    top = jnp.maximum(jnp.max(lse_all, axis=0), tree_lse)
    scale = jnp.exp(lse_all - top[None])
    tree_scale = jnp.exp(tree_lse - top)
    total = jnp.sum(scale, axis=0) + tree_scale
    joined = jnp.sum(scale * orecv[:, :, 0:CW].astype(f32), axis=0) + tree_scale * tree_out
    joined = joined / total
    for c in range(CHUNKS):
        for r in range(3):
            for k in range(2):
                at = c * CW + (k * 3 + r) * HEAD
                flat_s[0:TOK, at:at + HEAD] = (
                    joined[c * TOK:(c + 1) * TOK, (2 * r + k) * HEAD:(2 * r + k + 1) * HEAD]
                )
    attn = flat_s[0:TOK, :].astype(bf16)
    attn_ref[...] = attn

    loads[2].wait()
    hidden = res_s[0:TOK, :] + dot(attn, ow[...])
    mean = jnp.mean(hidden * hidden, axis=-1, keepdims=True)
    normed = (hidden * lax.rsqrt(mean + norm_eps) * gain_ref[...]).astype(bf16).astype(f32)
    for c in range(CHUNKS):
        chunk_s[c * TOK:(c + 1) * TOK, :] = normed[:, c * CW:(c + 1) * CW]
    nall[t] = chunk_s[...].astype(bf16)

    each(N_TP, lambda k: n_copy(k, t).start())
    expert_lane = iota((GROUP, EXPERTS), 1)
    ids = ids_ref[...]
    picked = expert_lane == ids[:, 0:1]
    for k in range(1, ids.shape[1]):
        picked = picked | (expert_lane == ids[:, k:k + 1])
    loads[3].wait()
    loads[4].wait()
    loads[5].wait()
    each(N_TP, lambda k: n_copy(k, tp_peer(k)).wait_recv())
    for s in range(2):
        rows = dot(perm_s[...], nall[s * HALF:(s + 1) * HALF].reshape(256, CW)).astype(bf16)
        for c in range(CHUNKS):
            nfull[s * DRAFT:(s + 1) * DRAFT, c * CW:(c + 1) * CW] = rows[c * DRAFT:(c + 1) * DRAFT]
    normed_all = nfull[...]
    expo = jnp.where(picked, jnp.exp(dot(normed_all, rw[...])), 0.0)
    routing = expo / jnp.sum(expo, axis=1, keepdims=True)
    for u in range(UNITS_DEV):
        expert = (t * UNITS_DEV + u) // (FF_E // UNIT)
        share = jnp.sum(jnp.where(expert_lane == expert, routing, 0.0), axis=1, keepdims=True)
        both = dot(normed_all, gu[u])
        gate = both[:, :UNIT]
        active = gate / (1.0 + jnp.exp(-gate)) * both[:, UNIT:] * share
        act_s[:, u * UNIT:(u + 1) * UNIT] = active.astype(bf16)
    moe = dot(act_s[...], dw[...].reshape(UNITS_DEV * UNIT, D)).astype(bf16)
    for s in range(2):
        for c in range(CHUNKS):
            moe_s[c * DRAFT:(c + 1) * DRAFT, :] = moe[s * DRAFT:(s + 1) * DRAFT, c * CW:(c + 1) * CW]
        msend[s * HALF:(s + 1) * HALF] = (
            dot(permt_s[...], moe_s[...]).astype(bf16).reshape(HALF, ROWS, CW)
        )

    each(N_TP, lambda k: m_copy(k, tp_peer(k), t).start())
    mrecv[t] = msend[t]
    each(N_REQ, lambda k: q8_copy(k, g).wait_send())
    each(N_REQ, lambda k: r8_copy(k, g).wait_send())
    each(N_TP, lambda k: q_copy(k, t).wait_send())
    each(HALF, lambda k: kv_copy(k, t_in).wait_send())
    each(N_TP, lambda k: o_copy(k, 0, t).wait_send())
    each(N_TP, lambda k: n_copy(k, t).wait_send())
    each(N_TP, lambda k: m_copy(k, 0, tp_peer(k)).wait_recv())
    moe_own = jnp.sum(mrecv[...].astype(f32), axis=0)
    for c in range(CHUNKS):
        flat_s[0:TOK, c * CW:(c + 1) * CW] = moe_own[c * TOK:(c + 1) * TOK, :]
    layer_ref[...] = (hidden + flat_s[0:TOK, :]).astype(bf16)
    each(N_TP, lambda k: m_copy(k, 0, t).wait_send())


def per_device(
    queries, new_kv, residual, placement, lengths, page_table, cache_keys, cache_values,
    parents, accept_leaf, out_weight, norm_gain, router_weight, expert_ids, gate_up, down_weight,
):
    smem = pl.BlockSpec(memory_space=pltpu.SMEM)
    vmem = pl.BlockSpec(memory_space=pltpu.VMEM)
    hbm = pl.BlockSpec(memory_space=pl.ANY)
    dma = pltpu.SemaphoreType.DMA
    return pl.pallas_call(
        kernel,
        out_shape=(
            jax.ShapeDtypeStruct((TOK, D), bf16),
            jax.ShapeDtypeStruct((TOK, D), bf16),
            jax.ShapeDtypeStruct((TOK, 1024), bf16),
        ),
        in_specs=[smem] * 4 + [vmem] * 6 + [hbm] * 6,
        out_specs=(vmem, vmem, vmem),
        scratch_shapes=[
            pltpu.VMEM((2, PAGE, 512), bf16),
            pltpu.VMEM((2, PAGE, 512), bf16),
            pltpu.VMEM((D, D), bf16),
            pltpu.VMEM((D, EXPERTS), bf16),
            pltpu.VMEM((UNITS_DEV, D, 2 * UNIT), bf16),
            pltpu.VMEM((UNITS_DEV, UNIT, D), bf16),
            pltpu.VMEM((N_REQ, ROWS, CW), bf16),
            pltpu.VMEM((N_REQ, ROWS, 640), bf16),
            pltpu.VMEM((N_TP, ROWS, CW), bf16),
            pltpu.VMEM((HALF, ROWS, 256), bf16),
            pltpu.VMEM((N_TP, ROWS, 512), bf16),
            pltpu.VMEM((N_TP, ROWS, 512), bf16),
            pltpu.VMEM((N_TP, ROWS, CW), bf16),
            pltpu.VMEM((N_TP, ROWS, CW), bf16),
            pltpu.VMEM((N_TP, ROWS, CW), bf16),
            pltpu.VMEM((ROWS, CW), f32),
            pltpu.VMEM((8, D), f32),
            pltpu.VMEM((8, D), f32),
            pltpu.VMEM((256, 256), bf16),
            pltpu.VMEM((256, 256), bf16),
            pltpu.VMEM((256, 512), bf16),
            pltpu.VMEM((GROUP, D), bf16),
            pltpu.VMEM((GROUP, UNITS_DEV * UNIT), bf16),
            pltpu.VMEM((256, CW), bf16),
            dma((6,)),
            dma((N_REQ,)), dma((N_REQ,)), dma((N_REQ,)), dma((N_REQ,)),
            dma((N_TP,)), dma((N_TP,)), dma((HALF,)), dma((HALF,)),
            dma((N_TP,)), dma((N_TP,)), dma((N_TP,)), dma((N_TP,)), dma((N_TP,)), dma((N_TP,)),
        ],
        compiler_params=pltpu.CompilerParams(
            collective_id=0, has_side_effects=True, vmem_limit_bytes=48 << 20
        ),
        name="verify_layer",
    )(
        placement, lengths, page_table.reshape(2), accept_leaf,
        queries, new_kv, residual, parents, norm_gain.reshape(1, D), expert_ids,
        cache_keys, cache_values, out_weight, router_weight, gate_up, down_weight,
    )


def solution(mesh):
    in_specs = (
        P(("req", "tp"), None),
        P(("req", "tp"), None),
        P(("req", "tp"), None),
        P("req"),
        P("req"),
        P("req", None, "tp"),
        P(("req", "tp"), None, None),
        P(("req", "tp"), None, None),
        P("req", None),
        P("req"),
        P(),
        P(),
        P(),
        P("req", None),
        P("tp", None, None),
        P("tp", None, None),
    )
    out_specs = (P(("req", "tp"), None), P(("req", "tp"), None), P(("req", "tp"), None))
    return jax.shard_map(
        per_device, mesh=mesh, in_specs=in_specs, out_specs=out_specs, check_vma=False
    )
```

```python
import jax
import jax.numpy as jnp
from jax import lax
from jax.experimental import pallas as pl
from jax.experimental.pallas import tpu as pltpu
from jax.sharding import PartitionSpec as P

HEADS = 24
KV_HEADS = 8
HEAD = 64
D = 1536
EXPERTS = 40
FF_E = 512
UNIT = 128
UNITS_DEV = 5
DRAFT = 64
PAGE = 128
N_REQ = 8
N_TP = 32
TOK = 4
CHUNKS = 4
CW = D // CHUNKS
HALF = N_TP // 2
ROWS = CHUNKS * TOK
GROUP = N_TP * TOK

neg_big = -1e30
norm_eps = 1e-06
MESH = pl.DeviceIdType.MESH
f32 = jnp.float32
bf16 = jnp.bfloat16


def iota(shape, dim):
    return lax.broadcasted_iota(jnp.int32, shape, dim)


def ones_at(mask):
    return jnp.where(mask, 1.0, 0.0).astype(bf16)


def dot(a, b):
    return jnp.dot(a, b, preferred_element_type=f32)


def dot_t(a, b):
    return lax.dot_general(a, b, (((1,), (1,)), ((), ())), preferred_element_type=f32)


def softmax_block(stacked, keys, values, lo, hi, ones_rhs, valid):
    count = keys.shape[0]
    keys_two = jnp.concatenate([keys * lo, keys * hi], axis=0)
    values_two = jnp.concatenate([values * lo, values * hi], axis=0)
    scores = dot_t(stacked, keys_two)
    s_lo = jnp.where(valid, scores[:, :count], neg_big)
    s_hi = jnp.where(valid, scores[:, count:], neg_big)
    m_lo = jnp.max(s_lo, axis=1, keepdims=True)
    m_hi = jnp.max(s_hi, axis=1, keepdims=True)
    w_lo = jnp.where(valid, jnp.exp(s_lo - m_lo), 0.0).astype(bf16)
    w_hi = jnp.where(valid, jnp.exp(s_hi - m_hi), 0.0).astype(bf16)
    weights = jnp.concatenate([w_lo, w_hi], axis=1)
    both = dot(weights, jnp.concatenate([values_two, ones_rhs], axis=1))
    out, total = both[:, :128], both[:, 128:]
    rows = out.shape[0]
    first = iota((rows, 128), 1) < HEAD
    top = jnp.where(first, m_lo, m_hi)
    some = total > 0.0
    safe = jnp.where(some, total, 1.0)
    return out / safe, jnp.where(some, top + jnp.log(safe), neg_big)


def two_ones(count):
    row = iota((2 * count, 128), 0)
    lane = iota((2 * count, 128), 1)
    return ones_at((row >= count) == (lane >= HEAD))


def kernel(
    q_hbm, kv_hbm, res_hbm, placement_hbm, lengths_hbm, table_hbm, keys_hbm, vals_hbm,
    par_hbm, leaf_hbm, ow_hbm, gain_hbm, rw_hbm, ids_hbm, gu_hbm, dw_hbm,
    attn_ref, layer_ref, acc_ref,
    q_ref, kv_ref, res_ref, placement, lengths, table, kbuf, vbuf,
    par_ref, leaf, ow, gain_ref, rw, ids_ref, gu, dw,
    q8, r8, qall, kvall, osend, orecv, nall, msend, mrecv,
    chunk_s, flat_s, res_s, perm_s, permt_s, outs_s, nfull, act_s, moe_s,
    wsem, s_q8, r_q8, s_r8, r_r8, s_q, r_q, s_kv, r_kv, s_o, r_o, s_n, r_n, s_m, r_m,
):
    g = lax.axis_index("req")
    t = lax.axis_index("tp")
    half = t // HALF
    t_in = t % HALF

    def req_peer(k):
        return lax.rem(g + k, N_REQ)

    def tp_peer(k):
        return lax.rem(t // 4 + k // 4, 8) * 4 + lax.rem(t % 4 + k % 4, 4)

    def slot_peer(k):
        return half * HALF + lax.rem(t_in + k, HALF)

    barrier = pltpu.get_barrier_semaphore()

    def greet_req(k, carry):
        pl.semaphore_signal(barrier, inc=1, device_id={"req": req_peer(k)}, device_id_type=MESH)
        return carry

    def greet_tp(k, carry):
        pl.semaphore_signal(barrier, inc=1, device_id={"tp": tp_peer(k)}, device_id_type=MESH)
        return carry

    def load(i, source, target):
        copy = pltpu.make_async_copy(source, target, wsem.at[i])
        copy.start()
        return copy

    load_q = load(0, q_hbm, q_ref)
    load_kv = load(1, kv_hbm, kv_ref)
    load_res = load(2, res_hbm, res_ref)
    lax.fori_loop(1, N_REQ, greet_req, 0)
    lax.fori_loop(1, N_TP, greet_tp, 0)
    load_placement = load(3, placement_hbm, placement)
    load_par = load(4, par_hbm, par_ref)
    load_leaf = load(5, leaf_hbm, leaf)
    load_lengths = load(6, lengths_hbm, lengths)
    load_table = load(7, table_hbm, table)
    load_keys = load(8, keys_hbm, kbuf)
    load_vals = load(9, vals_hbm, vbuf)
    load_gain = load(10, gain_hbm, gain_ref.at[0])
    load_ids = load(11, ids_hbm, ids_ref)
    load_rw = load(12, rw_hbm, rw)
    load_ow = load(13, ow_hbm, ow)
    load_gu = load(14, gu_hbm, gu)
    load_dw = load(15, dw_hbm, dw)

    load_q.wait()
    q_in = q_ref[...].astype(f32) * (HEAD ** -0.5)
    for c in range(CHUNKS):
        for r in range(3):
            for k in range(2):
                at = c * CW + (k * 3 + r) * HEAD
                chunk_s[c * TOK:(c + 1) * TOK, (2 * r + k) * HEAD:(2 * r + k + 1) * HEAD] = (
                    q_in[:, at:at + HEAD]
                )
    q8[g] = chunk_s[...].astype(bf16)
    load_kv.wait()
    kv_in = kv_ref[...].astype(f32)
    for c in range(CHUNKS):
        chunk_s[c * TOK:(c + 1) * TOK, 0:128] = kv_in[:, c * 128:(c + 1) * 128]
        chunk_s[c * TOK:(c + 1) * TOK, 128:256] = kv_in[:, 512 + c * 128:512 + (c + 1) * 128]
    r8[g, :, 0:256] = chunk_s[:, 0:256].astype(bf16)
    load_res.wait()
    res_in = res_ref[...].astype(f32)
    for c in range(CHUNKS):
        chunk_s[c * TOK:(c + 1) * TOK, :] = res_in[:, c * CW:(c + 1) * CW]
    r8[g, :, 256:640] = chunk_s[...].astype(bf16)

    def q8_copy(k, source):
        return pltpu.make_async_remote_copy(
            src_ref=q8.at[source], dst_ref=q8.at[source], send_sem=s_q8.at[k],
            recv_sem=r_q8.at[source], device_id={"req": req_peer(k)}, device_id_type=MESH,
        )

    def r8_copy(k, source):
        return pltpu.make_async_remote_copy(
            src_ref=r8.at[source], dst_ref=r8.at[source], send_sem=s_r8.at[k],
            recv_sem=r_r8.at[source], device_id={"req": req_peer(k)}, device_id_type=MESH,
        )

    def q_copy(k, source):
        return pltpu.make_async_remote_copy(
            src_ref=qall.at[source], dst_ref=qall.at[source], send_sem=s_q.at[k],
            recv_sem=r_q.at[source], device_id={"tp": tp_peer(k)}, device_id_type=MESH,
        )

    def kv_copy(k, source):
        return pltpu.make_async_remote_copy(
            src_ref=kvall.at[source], dst_ref=kvall.at[source], send_sem=s_kv.at[k],
            recv_sem=r_kv.at[source], device_id={"tp": slot_peer(k)}, device_id_type=MESH,
        )

    def o_copy(k, block, source):
        return pltpu.make_async_remote_copy(
            src_ref=osend.at[block], dst_ref=orecv.at[source], send_sem=s_o.at[k],
            recv_sem=r_o.at[source], device_id={"tp": tp_peer(k)}, device_id_type=MESH,
        )

    def n_copy(k, source):
        return pltpu.make_async_remote_copy(
            src_ref=nall.at[source], dst_ref=nall.at[source], send_sem=s_n.at[k],
            recv_sem=r_n.at[source], device_id={"tp": tp_peer(k)}, device_id_type=MESH,
        )

    def m_copy(k, block, source):
        return pltpu.make_async_remote_copy(
            src_ref=msend.at[block], dst_ref=mrecv.at[source], send_sem=s_m.at[k],
            recv_sem=r_m.at[source], device_id={"tp": tp_peer(k)}, device_id_type=MESH,
        )

    def each(count, step):
        def body(k, carry):
            step(k)
            return carry

        lax.fori_loop(1, count, body, 0)

    row_a = iota((256, 256), 0)
    row_b = iota((256, 256), 1)
    perm_s[...] = ones_at(
        row_b == ((row_a & 63) >> 2) * ROWS + (row_a >> 6) * TOK + (row_a & 3)
    )
    permt_s[...] = ones_at(
        row_a == ((row_b & 63) >> 2) * ROWS + (row_b >> 6) * TOK + (row_b & 3)
    )

    pl.semaphore_wait(barrier, N_REQ - 1 + N_TP - 1)

    each(N_REQ, lambda k: q8_copy(k, g).start())
    each(N_REQ, lambda k: r8_copy(k, g).start())

    node_m = iota((DRAFT, DRAFT), 0)
    node_n = iota((DRAFT, DRAFT), 1)
    load_par.wait()
    load_leaf.wait()
    parent_row = par_ref[pl.ds(half, 1), :]
    reach_t = ones_at(((node_m == parent_row) & (node_n > 0)) | (node_m == node_n))
    for _ in range(6):
        reach_t = jnp.minimum(dot(reach_t, reach_t), 1.0).astype(bf16)
    own_node = t_in * TOK + (iota((ROWS, DRAFT), 0) & 3)
    lane_node = iota((ROWS, DRAFT), 1)
    spread_row = iota((DRAFT, 256), 0)
    spread_lane = iota((DRAFT, 256), 1)
    spread = ones_at(spread_row == (spread_lane >> 4) * TOK + (spread_lane & 3))
    same_chunk = ((iota((ROWS, 256), 1) >> 2) & 3) == (iota((ROWS, 256), 0) >> 2)
    own_reach = dot_t(ones_at(lane_node == own_node), reach_t).astype(bf16)
    tree_mask = jnp.where(same_chunk, dot(own_reach, spread), 0.0)
    flags = dot_t(ones_at(lane_node == leaf[half]), reach_t)
    rank = dot(flags.astype(bf16), ones_at(node_m <= node_n)) - 1.0
    chosen = ones_at((flags > 0.5) & (rank == own_node.astype(f32)))
    choice = jnp.where(same_chunk, dot(chosen, spread), 0.0).astype(bf16)

    lane_one = iota((1, 128), 1)
    lo = ones_at(lane_one < HEAD)
    hi = ones_at(lane_one >= HEAD)

    each(N_REQ, lambda k: q8_copy(k, req_peer(k)).wait_recv())
    load_placement.wait()
    source_group = lax.shift_right_logical(placement[half], 1)
    own_q = q8[source_group]
    qall[t] = own_q
    each(N_TP, lambda k: q_copy(k, t).start())
    each(N_REQ, lambda k: r8_copy(k, req_peer(k)).wait_recv())
    own_kvres = r8[source_group]
    kvall[t_in] = own_kvres[:, 0:256]
    each(HALF, lambda k: kv_copy(k, t_in).start())
    own_res = own_kvres[:, 256:640].astype(f32)
    for c in range(CHUNKS):
        res_s[0:TOK, c * CW:(c + 1) * CW] = own_res[c * TOK:(c + 1) * TOK, :]

    ones_page = two_ones(PAGE)
    load_lengths.wait()
    load_table.wait()
    load_keys.wait()
    load_vals.wait()
    each(N_TP, lambda k: q_copy(k, tp_peer(k)).wait_recv())
    stat_lane = iota((DRAFT, 128), 1)
    piece = stat_lane & 7
    stat_r = (stat_lane & 63) >> 3
    for s in range(2):
        q_slot = dot(perm_s[...], qall[s * HALF:(s + 1) * HALF].reshape(256, CW)).astype(bf16)
        page = table[s]
        page_k = kbuf[page]
        page_v = vbuf[page]
        valid = t * PAGE + iota((1, PAGE), 1) < lengths[s]
        for c in range(CHUNKS):
            q_c = q_slot[c * DRAFT:(c + 1) * DRAFT]
            stacked = jnp.concatenate([q_c[:, r * 128:(r + 1) * 128] for r in range(3)], axis=0)
            out, lse = softmax_block(
                stacked, page_k[:, c * 128:(c + 1) * 128], page_v[:, c * 128:(c + 1) * 128],
                lo, hi, ones_page, valid,
            )
            stats = jnp.zeros((DRAFT, 128), f32)
            for r in range(3):
                outs_s[c * DRAFT:(c + 1) * DRAFT, r * 128:(r + 1) * 128] = (
                    out[r * DRAFT:(r + 1) * DRAFT].astype(bf16)
                )
                part = lse[r * DRAFT:(r + 1) * DRAFT]
                first = part.astype(bf16).astype(f32)
                rest = part - first
                second = rest.astype(bf16).astype(f32)
                third = rest - second
                value = jnp.where(piece == 0, first, jnp.where(piece == 1, second, third))
                stats = jnp.where((stat_r == r) & (piece < 3), value, stats)
            outs_s[c * DRAFT:(c + 1) * DRAFT, CW:512] = stats.astype(bf16)
        osend[s * HALF:(s + 1) * HALF] = (
            dot(permt_s[...], outs_s[...]).astype(bf16).reshape(HALF, ROWS, 512)
        )

    each(N_TP, lambda k: o_copy(k, tp_peer(k), t).start())
    orecv[t] = osend[t]

    each(HALF, lambda k: kv_copy(k, lax.rem(t_in + k, HALF)).wait_recv())
    kv_slot = kvall[...].reshape(256, 256)
    accepted = dot(choice, kv_slot)
    for c in range(CHUNKS):
        acc_ref[:, c * 128:(c + 1) * 128] = accepted[c * TOK:(c + 1) * TOK, 0:128].astype(bf16)
        acc_ref[:, 512 + c * 128:512 + (c + 1) * 128] = (
            accepted[c * TOK:(c + 1) * TOK, 128:256].astype(bf16)
        )
    q_own = jnp.concatenate([own_q[:, r * 128:(r + 1) * 128] for r in range(3)], axis=0)
    tree_valid = jnp.concatenate([tree_mask] * 3, axis=0) > 0.5
    tree_out, tree_lse = softmax_block(
        q_own, kv_slot[:, 0:128], kv_slot[:, 128:256], lo, hi, two_ones(256), tree_valid
    )
    tree_out = jnp.concatenate([tree_out[r * ROWS:(r + 1) * ROWS] for r in range(3)], axis=1)
    tree_lse = jnp.concatenate([tree_lse[r * ROWS:(r + 1) * ROWS] for r in range(3)], axis=1)
    ex_l = iota((128, CW), 0)
    ex_c = iota((128, CW), 1)
    expand = ones_at(
        ((ex_l >> 6) == ((ex_c >> 6) & 1)) & (((ex_l & 63) >> 3) == (ex_c >> 7)) & ((ex_l & 7) < 3)
    )

    each(N_TP, lambda k: o_copy(k, 0, tp_peer(k)).wait_recv())
    lse_all = dot(orecv[:, :, CW:512].reshape(N_TP * ROWS, 128), expand).reshape(N_TP, ROWS, CW)
    top = jnp.maximum(jnp.max(lse_all, axis=0), tree_lse)
    scale = jnp.exp(lse_all - top[None])
    tree_scale = jnp.exp(tree_lse - top)
    total = jnp.sum(scale, axis=0) + tree_scale
    joined = jnp.sum(scale * orecv[:, :, 0:CW].astype(f32), axis=0) + tree_scale * tree_out
    joined = joined / total
    for c in range(CHUNKS):
        for r in range(3):
            for k in range(2):
                at = c * CW + (k * 3 + r) * HEAD
                flat_s[0:TOK, at:at + HEAD] = (
                    joined[c * TOK:(c + 1) * TOK, (2 * r + k) * HEAD:(2 * r + k + 1) * HEAD]
                )
    attn = flat_s[0:TOK, :].astype(bf16)
    attn_ref[...] = attn

    load_ow.wait()
    load_gain.wait()
    hidden = res_s[0:TOK, :] + dot(attn, ow[...])
    mean = jnp.mean(hidden * hidden, axis=-1, keepdims=True)
    normed = (hidden * lax.rsqrt(mean + norm_eps) * gain_ref[...]).astype(bf16).astype(f32)
    for c in range(CHUNKS):
        chunk_s[c * TOK:(c + 1) * TOK, :] = normed[:, c * CW:(c + 1) * CW]
    nall[t] = chunk_s[...].astype(bf16)

    each(N_TP, lambda k: n_copy(k, t).start())
    expert_row = iota((EXPERTS, GROUP), 0)
    load_ids.wait()
    ids = ids_ref[...]
    picked = expert_row == ids[0:1]
    for k in range(1, ids.shape[0]):
        picked = picked | (expert_row == ids[k:k + 1])
    load_rw.wait()
    load_gu.wait()
    load_dw.wait()
    each(N_TP, lambda k: n_copy(k, tp_peer(k)).wait_recv())
    for s in range(2):
        rows = dot(perm_s[...], nall[s * HALF:(s + 1) * HALF].reshape(256, CW)).astype(bf16)
        for c in range(CHUNKS):
            nfull[s * DRAFT:(s + 1) * DRAFT, c * CW:(c + 1) * CW] = rows[c * DRAFT:(c + 1) * DRAFT]
    normed_all = nfull[...]
    expo = jnp.where(picked, jnp.exp(dot_t(rw[...], normed_all)), 0.0)
    routing = expo / jnp.sum(expo, axis=0, keepdims=True)
    first_expert = t * UNITS_DEV // (FF_E // UNIT)
    two = jnp.concatenate(
        [
            jnp.sum(jnp.where(expert_row == first_expert + k, routing, 0.0), axis=0, keepdims=True)
            for k in range(2)
        ]
        + [jnp.zeros((GROUP - 2, GROUP), f32)],
        axis=0,
    )
    columns = jnp.transpose(two)
    for u in range(UNITS_DEV):
        same = (t * UNITS_DEV + u) // (FF_E // UNIT) == first_expert
        share = jnp.where(same, columns[:, 0:1], columns[:, 1:2])
        both = dot(normed_all, gu[u])
        gate = both[:, :UNIT]
        active = gate / (1.0 + jnp.exp(-gate)) * both[:, UNIT:] * share
        act_s[:, u * UNIT:(u + 1) * UNIT] = active.astype(bf16)
    moe = dot(act_s[...], dw[...].reshape(UNITS_DEV * UNIT, D)).astype(bf16)
    for s in range(2):
        for c in range(CHUNKS):
            moe_s[c * DRAFT:(c + 1) * DRAFT, :] = moe[s * DRAFT:(s + 1) * DRAFT, c * CW:(c + 1) * CW]
        msend[s * HALF:(s + 1) * HALF] = (
            dot(permt_s[...], moe_s[...]).astype(bf16).reshape(HALF, ROWS, CW)
        )

    each(N_TP, lambda k: m_copy(k, tp_peer(k), t).start())
    mrecv[t] = msend[t]
    each(N_REQ, lambda k: q8_copy(k, g).wait_send())
    each(N_REQ, lambda k: r8_copy(k, g).wait_send())
    each(N_TP, lambda k: q_copy(k, t).wait_send())
    each(HALF, lambda k: kv_copy(k, t_in).wait_send())
    each(N_TP, lambda k: o_copy(k, 0, t).wait_send())
    each(N_TP, lambda k: n_copy(k, t).wait_send())
    each(N_TP, lambda k: m_copy(k, 0, tp_peer(k)).wait_recv())
    moe_own = jnp.sum(mrecv[...].astype(f32), axis=0)
    for c in range(CHUNKS):
        flat_s[0:TOK, c * CW:(c + 1) * CW] = moe_own[c * TOK:(c + 1) * TOK, :]
    layer_ref[...] = (hidden + flat_s[0:TOK, :]).astype(bf16)
    each(N_TP, lambda k: m_copy(k, 0, t).wait_send())


def per_device(
    queries, new_kv, residual, placement, lengths, page_table, cache_keys, cache_values,
    parents, accept_leaf, out_weight, norm_gain, router_weight, expert_ids, gate_up, down_weight,
):
    vmem = pl.BlockSpec(memory_space=pltpu.VMEM)
    hbm = pl.BlockSpec(memory_space=pltpu.MemorySpace.HBM)
    dma = pltpu.SemaphoreType.DMA
    return pl.pallas_call(
        kernel,
        out_shape=(
            jax.ShapeDtypeStruct((TOK, D), bf16),
            jax.ShapeDtypeStruct((TOK, D), bf16),
            jax.ShapeDtypeStruct((TOK, 1024), bf16),
        ),
        in_specs=[hbm] * 16,
        out_specs=(vmem, vmem, vmem),
        scratch_shapes=[
            pltpu.VMEM((TOK, D), bf16),
            pltpu.VMEM((TOK, 1024), bf16),
            pltpu.VMEM((TOK, D), bf16),
            pltpu.SMEM((2,), jnp.int32),
            pltpu.SMEM((2,), jnp.int32),
            pltpu.SMEM((2,), jnp.int32),
            pltpu.VMEM((2, PAGE, 512), bf16),
            pltpu.VMEM((2, PAGE, 512), bf16),
            pltpu.VMEM((2, DRAFT), jnp.int32),
            pltpu.SMEM((2,), jnp.int32),
            pltpu.VMEM((D, D), bf16),
            pltpu.VMEM((1, D), f32),
            pltpu.VMEM((EXPERTS, D), bf16),
            pltpu.VMEM((8, GROUP), jnp.int32),
            pltpu.VMEM((UNITS_DEV, D, 2 * UNIT), bf16),
            pltpu.VMEM((UNITS_DEV, UNIT, D), bf16),
            pltpu.VMEM((N_REQ, ROWS, CW), bf16),
            pltpu.VMEM((N_REQ, ROWS, 640), bf16),
            pltpu.VMEM((N_TP, ROWS, CW), bf16),
            pltpu.VMEM((HALF, ROWS, 256), bf16),
            pltpu.VMEM((N_TP, ROWS, 512), bf16),
            pltpu.VMEM((N_TP, ROWS, 512), bf16),
            pltpu.VMEM((N_TP, ROWS, CW), bf16),
            pltpu.VMEM((N_TP, ROWS, CW), bf16),
            pltpu.VMEM((N_TP, ROWS, CW), bf16),
            pltpu.VMEM((ROWS, CW), f32),
            pltpu.VMEM((8, D), f32),
            pltpu.VMEM((8, D), f32),
            pltpu.VMEM((256, 256), bf16),
            pltpu.VMEM((256, 256), bf16),
            pltpu.VMEM((256, 512), bf16),
            pltpu.VMEM((GROUP, D), bf16),
            pltpu.VMEM((GROUP, UNITS_DEV * UNIT), bf16),
            pltpu.VMEM((256, CW), bf16),
            dma((16,)),
            dma((N_REQ,)), dma((N_REQ,)), dma((N_REQ,)), dma((N_REQ,)),
            dma((N_TP,)), dma((N_TP,)), dma((HALF,)), dma((HALF,)),
            dma((N_TP,)), dma((N_TP,)), dma((N_TP,)), dma((N_TP,)), dma((N_TP,)), dma((N_TP,)),
        ],
        compiler_params=pltpu.CompilerParams(
            collective_id=0, has_side_effects=True, vmem_limit_bytes=64 << 20
        ),
        name="verify_layer",
    )(
        queries, new_kv, residual, placement, lengths, page_table.reshape(2),
        cache_keys, cache_values, parents, accept_leaf, out_weight, norm_gain,
        router_weight.T, expert_ids.T, gate_up, down_weight,
    )


def solution(mesh):
    in_specs = (
        P(("req", "tp"), None),
        P(("req", "tp"), None),
        P(("req", "tp"), None),
        P("req"),
        P("req"),
        P("req", None, "tp"),
        P(("req", "tp"), None, None),
        P(("req", "tp"), None, None),
        P("req", None),
        P("req"),
        P(),
        P(),
        P(),
        P("req", None),
        P("tp", None, None),
        P("tp", None, None),
    )
    out_specs = (P(("req", "tp"), None), P(("req", "tp"), None), P(("req", "tp"), None))
    return jax.shard_map(
        per_device, mesh=mesh, in_specs=in_specs, out_specs=out_specs, check_vma=False
    )
```

```python
import jax
import jax.numpy as jnp
from jax import lax
from jax.experimental import pallas as pl
from jax.experimental.pallas import tpu as pltpu
from jax.sharding import PartitionSpec as P

HEADS = 24
KV_HEADS = 8
HEAD = 64
D = 1536
EXPERTS = 40
FF_E = 512
UNIT = 128
UNITS_DEV = 5
DRAFT = 64
PAGE = 128
N_REQ = 8
N_TP = 32
TOK = 4
CHUNKS = 4
CW = D // CHUNKS
HALF = N_TP // 2
ROWS = CHUNKS * TOK
GROUP = N_TP * TOK

neg_big = -1e30
norm_eps = 1e-06
MESH = pl.DeviceIdType.MESH
f32 = jnp.float32
bf16 = jnp.bfloat16


def iota(shape, dim):
    return lax.broadcasted_iota(jnp.int32, shape, dim)


def ones_at(mask):
    return jnp.where(mask, 1.0, 0.0).astype(bf16)


def dot(a, b):
    return jnp.dot(a, b, preferred_element_type=f32)


def dot_t(a, b):
    return lax.dot_general(a, b, (((1,), (1,)), ((), ())), preferred_element_type=f32)


def softmax_block(stacked, keys, values, lo, hi, ones_rhs, valid):
    count = keys.shape[0]
    keys_two = jnp.concatenate([keys * lo, keys * hi], axis=0)
    values_two = jnp.concatenate([values * lo, values * hi], axis=0)
    scores = dot_t(stacked, keys_two)
    s_lo = jnp.where(valid, scores[:, :count], neg_big)
    s_hi = jnp.where(valid, scores[:, count:], neg_big)
    m_lo = jnp.max(s_lo, axis=1, keepdims=True)
    m_hi = jnp.max(s_hi, axis=1, keepdims=True)
    w_lo = jnp.where(valid, jnp.exp(s_lo - m_lo), 0.0).astype(bf16)
    w_hi = jnp.where(valid, jnp.exp(s_hi - m_hi), 0.0).astype(bf16)
    weights = jnp.concatenate([w_lo, w_hi], axis=1)
    both = dot(weights, jnp.concatenate([values_two, ones_rhs], axis=1))
    out, total = both[:, :128], both[:, 128:]
    rows = out.shape[0]
    first = iota((rows, 128), 1) < HEAD
    top = jnp.where(first, m_lo, m_hi)
    some = total > 0.0
    safe = jnp.where(some, total, 1.0)
    return out / safe, jnp.where(some, top + jnp.log(safe), neg_big)


def two_ones(count):
    row = iota((2 * count, 128), 0)
    lane = iota((2 * count, 128), 1)
    return ones_at((row >= count) == (lane >= HEAD))


def kernel(
    q_hbm, kv_hbm, res_hbm, placement_hbm, lengths_hbm, table_hbm, keys_hbm, vals_hbm,
    par_hbm, leaf_hbm, ow_hbm, gain_hbm, rw_hbm, ids_hbm, gu_hbm, dw_hbm,
    attn_ref, layer_ref, acc_ref,
    q_ref, kv_ref, res_ref, placement, lengths, table, kbuf, vbuf,
    par_ref, leaf, ow, gain_ref, rw, ids_ref, gu, dw,
    q8, r8, qown, qall, kvall, pages_send, pages, osend, orecv, nall, msend, mrecv,
    heads_s, chunk_s, flat_s, res_s, perm_s, permt_s, nfull, act_s, moe_s,
    wsem, s_p, r_p, s_q8, r_q8, s_r8, r_r8, s_q, r_q, s_kv, r_kv, s_o, r_o, s_n, r_n, s_m, r_m,
):
    g = lax.axis_index("req")
    t = lax.axis_index("tp")
    x = t % 4
    row_start = t - x
    half = t // HALF
    t_in = t % HALF

    def req_peer(k):
        return lax.rem(g + k, N_REQ)

    def tp_peer(k):
        return lax.rem(t // 4 + k // 4, 8) * 4 + lax.rem(t % 4 + k % 4, 4)

    def slot_peer(k):
        return half * HALF + lax.rem(t_in + k, HALF)

    barrier = pltpu.get_barrier_semaphore()

    def greet_req(k, carry):
        pl.semaphore_signal(barrier, inc=1, device_id={"req": req_peer(k)}, device_id_type=MESH)
        return carry

    def greet_tp(k, carry):
        pl.semaphore_signal(barrier, inc=1, device_id={"tp": tp_peer(k)}, device_id_type=MESH)
        return carry

    def load(i, source, target):
        copy = pltpu.make_async_copy(source, target, wsem.at[i])
        copy.start()
        return copy

    load_q = load(0, q_hbm, q_ref)
    load_kv = load(1, kv_hbm, kv_ref)
    load_res = load(2, res_hbm, res_ref)
    lax.fori_loop(1, N_REQ, greet_req, 0)
    lax.fori_loop(1, N_TP, greet_tp, 0)
    load_placement = load(3, placement_hbm, placement)
    load_par = load(4, par_hbm, par_ref)
    load_leaf = load(5, leaf_hbm, leaf)
    load_lengths = load(6, lengths_hbm, lengths)
    load_table = load(7, table_hbm, table)
    load_keys = load(8, keys_hbm, kbuf)
    load_vals = load(9, vals_hbm, vbuf)
    load_gain = load(10, gain_hbm, gain_ref.at[0])
    load_ids = load(11, ids_hbm, ids_ref)
    load_rw = load(12, rw_hbm, rw)
    load_ow = load(13, ow_hbm, ow)
    load_gu = load(14, gu_hbm, gu)
    load_dw = load(15, dw_hbm, dw)

    load_q.wait()
    q_in = q_ref[...].astype(f32) * (HEAD ** -0.5)
    heads_s[...] = jnp.zeros_like(heads_s)
    for c in range(CHUNKS):
        for r in range(3):
            for k in range(2):
                at = c * CW + (k * 3 + r) * HEAD
                row = c * ROWS + r * TOK
                heads_s[row:row + TOK, k * HEAD:(k + 1) * HEAD] = q_in[:, at:at + HEAD]
    q8[g] = heads_s[...].astype(bf16).reshape(CHUNKS, ROWS, 128)
    load_kv.wait()
    kv_in = kv_ref[...].astype(f32)
    for c in range(CHUNKS):
        chunk_s[c * TOK:(c + 1) * TOK, 0:128] = kv_in[:, c * 128:(c + 1) * 128]
        chunk_s[c * TOK:(c + 1) * TOK, 128:256] = kv_in[:, 512 + c * 128:512 + (c + 1) * 128]
    r8[g, :, 0:256] = chunk_s[:, 0:256].astype(bf16)
    load_res.wait()
    res_in = res_ref[...].astype(f32)
    for c in range(CHUNKS):
        chunk_s[c * TOK:(c + 1) * TOK, :] = res_in[:, c * CW:(c + 1) * CW]
    r8[g, :, 256:640] = chunk_s[...].astype(bf16)

    def page_copy(k, source):
        peer = lax.rem(x + k, 4)
        return pltpu.make_async_remote_copy(
            src_ref=pages_send.at[peer], dst_ref=pages.at[source], send_sem=s_p.at[k],
            recv_sem=r_p.at[source], device_id={"tp": row_start + peer}, device_id_type=MESH,
        )

    def q8_copy(k, source):
        return pltpu.make_async_remote_copy(
            src_ref=q8.at[source], dst_ref=q8.at[source], send_sem=s_q8.at[k],
            recv_sem=r_q8.at[source], device_id={"req": req_peer(k)}, device_id_type=MESH,
        )

    def r8_copy(k, source):
        return pltpu.make_async_remote_copy(
            src_ref=r8.at[source], dst_ref=r8.at[source], send_sem=s_r8.at[k],
            recv_sem=r_r8.at[source], device_id={"req": req_peer(k)}, device_id_type=MESH,
        )

    def q_copy(k, source):
        return pltpu.make_async_remote_copy(
            src_ref=qown.at[lax.rem(x + k % 4, 4)], dst_ref=qall.at[source], send_sem=s_q.at[k],
            recv_sem=r_q.at[source], device_id={"tp": tp_peer(k)}, device_id_type=MESH,
        )

    def kv_copy(k, source):
        return pltpu.make_async_remote_copy(
            src_ref=kvall.at[source], dst_ref=kvall.at[source], send_sem=s_kv.at[k],
            recv_sem=r_kv.at[source], device_id={"tp": slot_peer(k)}, device_id_type=MESH,
        )

    def o_copy(k, block, source):
        return pltpu.make_async_remote_copy(
            src_ref=osend.at[block], dst_ref=orecv.at[source], send_sem=s_o.at[k],
            recv_sem=r_o.at[source], device_id={"tp": tp_peer(k)}, device_id_type=MESH,
        )

    def n_copy(k, source):
        return pltpu.make_async_remote_copy(
            src_ref=nall.at[source], dst_ref=nall.at[source], send_sem=s_n.at[k],
            recv_sem=r_n.at[source], device_id={"tp": tp_peer(k)}, device_id_type=MESH,
        )

    def m_copy(k, block, source):
        return pltpu.make_async_remote_copy(
            src_ref=msend.at[block], dst_ref=mrecv.at[source], send_sem=s_m.at[k],
            recv_sem=r_m.at[source], device_id={"tp": tp_peer(k)}, device_id_type=MESH,
        )

    def each(count, step):
        def body(k, carry):
            step(k)
            return carry

        lax.fori_loop(1, count, body, 0)

    row_a = iota((256, 256), 0)
    row_b = iota((256, 256), 1)
    perm_s[...] = ones_at(
        row_b == ((row_a & 63) >> 2) * ROWS + (row_a >> 6) * TOK + (row_a & 3)
    )
    permt_s[...] = ones_at(
        row_a == ((row_b & 63) >> 2) * ROWS + (row_b >> 6) * TOK + (row_b & 3)
    )

    pl.semaphore_wait(barrier, N_REQ - 1 + N_TP - 1)

    each(N_REQ, lambda k: q8_copy(k, g).start())
    each(N_REQ, lambda k: r8_copy(k, g).start())

    load_table.wait()
    load_keys.wait()
    load_vals.wait()
    for s in range(2):
        page_k = kbuf[table[s]]
        page_v = vbuf[table[s]]
        for c in range(CHUNKS):
            pages_send[c, s] = page_k[:, c * 128:(c + 1) * 128]
            pages_send[c, 2 + s] = page_v[:, c * 128:(c + 1) * 128]
    each(4, lambda k: page_copy(k, x).start())
    pages[x] = pages_send[x]

    node_m = iota((DRAFT, DRAFT), 0)
    node_n = iota((DRAFT, DRAFT), 1)
    load_par.wait()
    load_leaf.wait()
    parent_row = par_ref[pl.ds(half, 1), :]
    reach_t = ones_at(((node_m == parent_row) & (node_n > 0)) | (node_m == node_n))
    for _ in range(6):
        reach_t = jnp.minimum(dot(reach_t, reach_t), 1.0).astype(bf16)
    own_node = t_in * TOK + (iota((ROWS, DRAFT), 0) & 3)
    lane_node = iota((ROWS, DRAFT), 1)
    tree_node = t_in * TOK + (iota((CHUNKS * ROWS, DRAFT), 0) & 3)
    tree_lane = iota((CHUNKS * ROWS, DRAFT), 1)
    spread_row = iota((DRAFT, 256), 0)
    spread_lane = iota((DRAFT, 256), 1)
    spread = ones_at(spread_row == (spread_lane >> 4) * TOK + (spread_lane & 3))
    same_chunk = ((iota((ROWS, 256), 1) >> 2) & 3) == (iota((ROWS, 256), 0) >> 2)
    tree_chunk = ((iota((CHUNKS * ROWS, 256), 1) >> 2) & 3) == (iota((CHUNKS * ROWS, 256), 0) >> 4)
    own_reach = dot_t(ones_at(tree_lane == tree_node), reach_t).astype(bf16)
    tree_valid = jnp.where(tree_chunk, dot(own_reach, spread), 0.0) > 0.5
    flags = dot_t(ones_at(lane_node == leaf[half]), reach_t)
    rank = dot(flags.astype(bf16), ones_at(node_m <= node_n)) - 1.0
    chosen = ones_at((flags > 0.5) & (rank == own_node.astype(f32)))
    choice = jnp.where(same_chunk, dot(chosen, spread), 0.0).astype(bf16)

    lane_one = iota((1, 128), 1)
    lo = ones_at(lane_one < HEAD)
    hi = ones_at(lane_one >= HEAD)

    each(N_REQ, lambda k: q8_copy(k, req_peer(k)).wait_recv())
    load_placement.wait()
    source_group = lax.shift_right_logical(placement[half], 1)
    own_q = q8[source_group]
    qown[...] = own_q
    qall[t] = qown[x]
    each(N_TP, lambda k: q_copy(k, t).start())
    each(N_REQ, lambda k: r8_copy(k, req_peer(k)).wait_recv())
    own_kvres = r8[source_group]
    kvall[t_in] = own_kvres[:, 0:256]
    each(HALF, lambda k: kv_copy(k, t_in).start())
    own_res = own_kvres[:, 256:640].astype(f32)
    for c in range(CHUNKS):
        res_s[0:TOK, c * CW:(c + 1) * CW] = own_res[c * TOK:(c + 1) * TOK, :]

    span = 4 * PAGE
    ones_page = two_ones(span)
    stat_lane = iota((256, 128), 1) & (HEAD - 1)
    load_lengths.wait()
    each(4, lambda k: page_copy(k, lax.rem(x + k, 4)).wait_recv())
    each(N_TP, lambda k: q_copy(k, tp_peer(k)).wait_recv())
    for s in range(2):
        valid = row_start * PAGE + iota((1, span), 1) < lengths[s]
        out, lse = softmax_block(
            qall[s * HALF:(s + 1) * HALF].reshape(256, 128), pages[:, s].reshape(span, 128),
            pages[:, 2 + s].reshape(span, 128), lo, hi, ones_page, valid,
        )
        first = lse.astype(bf16).astype(f32)
        rest = lse - first
        second = rest.astype(bf16).astype(f32)
        stats = jnp.where(stat_lane == 0, first, jnp.where(stat_lane == 1, second, rest - second))
        osend[s * HALF:(s + 1) * HALF, :, 0:128] = out.astype(bf16).reshape(HALF, ROWS, 128)
        osend[s * HALF:(s + 1) * HALF, :, 128:256] = stats.astype(bf16).reshape(HALF, ROWS, 128)

    each(N_TP, lambda k: o_copy(k, tp_peer(k), t).start())
    orecv[t] = osend[t]

    each(HALF, lambda k: kv_copy(k, lax.rem(t_in + k, HALF)).wait_recv())
    kv_slot = kvall[...].reshape(256, 256)
    accepted = dot(choice, kv_slot)
    for c in range(CHUNKS):
        acc_ref[:, c * 128:(c + 1) * 128] = accepted[c * TOK:(c + 1) * TOK, 0:128].astype(bf16)
        acc_ref[:, 512 + c * 128:512 + (c + 1) * 128] = (
            accepted[c * TOK:(c + 1) * TOK, 128:256].astype(bf16)
        )
    tree_out, tree_lse = softmax_block(
        own_q.reshape(CHUNKS * ROWS, 128), kv_slot[:, 0:128], kv_slot[:, 128:256], lo, hi,
        two_ones(256), tree_valid,
    )
    ex_row = iota((128, 128), 0)
    expand = ones_at(((ex_row >> 6) == (iota((128, 128), 1) >> 6)) & ((ex_row & (HEAD - 1)) < 3))

    each(N_TP, lambda k: o_copy(k, 0, tp_peer(k)).wait_recv())
    lse_all = dot(orecv[:, :, 128:256].reshape(N_TP * ROWS, 128), expand)
    lse_all = lse_all.reshape(N_TP // 4, CHUNKS * ROWS, 128)
    out_all = orecv[:, :, 0:128].reshape(N_TP // 4, CHUNKS * ROWS, 128).astype(f32)
    top = jnp.maximum(jnp.max(lse_all, axis=0), tree_lse)
    scale = jnp.exp(lse_all - top[None])
    tree_scale = jnp.exp(tree_lse - top)
    total = jnp.sum(scale, axis=0) + tree_scale
    joined = (jnp.sum(scale * out_all, axis=0) + tree_scale * tree_out) / total
    for c in range(CHUNKS):
        for r in range(3):
            for k in range(2):
                at = c * CW + (k * 3 + r) * HEAD
                row = c * ROWS + r * TOK
                flat_s[0:TOK, at:at + HEAD] = joined[row:row + TOK, k * HEAD:(k + 1) * HEAD]
    attn = flat_s[0:TOK, :].astype(bf16)
    attn_ref[...] = attn

    load_ow.wait()
    load_gain.wait()
    hidden = res_s[0:TOK, :] + dot(attn, ow[...])
    mean = jnp.mean(hidden * hidden, axis=-1, keepdims=True)
    normed = (hidden * lax.rsqrt(mean + norm_eps) * gain_ref[...]).astype(bf16).astype(f32)
    for c in range(CHUNKS):
        chunk_s[c * TOK:(c + 1) * TOK, :] = normed[:, c * CW:(c + 1) * CW]
    nall[t] = chunk_s[...].astype(bf16)

    each(N_TP, lambda k: n_copy(k, t).start())
    expert_row = iota((EXPERTS, GROUP), 0)
    load_ids.wait()
    ids = ids_ref[...]
    picked = expert_row == ids[0:1]
    for k in range(1, ids.shape[0]):
        picked = picked | (expert_row == ids[k:k + 1])
    load_rw.wait()
    load_gu.wait()
    load_dw.wait()
    each(N_TP, lambda k: n_copy(k, tp_peer(k)).wait_recv())
    for s in range(2):
        rows = dot(perm_s[...], nall[s * HALF:(s + 1) * HALF].reshape(256, CW)).astype(bf16)
        for c in range(CHUNKS):
            nfull[s * DRAFT:(s + 1) * DRAFT, c * CW:(c + 1) * CW] = rows[c * DRAFT:(c + 1) * DRAFT]
    normed_all = nfull[...]
    expo = jnp.where(picked, jnp.exp(dot_t(rw[...], normed_all)), 0.0)
    routing = expo / jnp.sum(expo, axis=0, keepdims=True)
    first_expert = t * UNITS_DEV // (FF_E // UNIT)
    two = jnp.concatenate(
        [
            jnp.sum(jnp.where(expert_row == first_expert + k, routing, 0.0), axis=0, keepdims=True)
            for k in range(2)
        ]
        + [jnp.zeros((GROUP - 2, GROUP), f32)],
        axis=0,
    )
    columns = jnp.transpose(two)
    for u in range(UNITS_DEV):
        same = (t * UNITS_DEV + u) // (FF_E // UNIT) == first_expert
        share = jnp.where(same, columns[:, 0:1], columns[:, 1:2])
        both = dot(normed_all, gu[u])
        gate = both[:, :UNIT]
        active = gate / (1.0 + jnp.exp(-gate)) * both[:, UNIT:] * share
        act_s[:, u * UNIT:(u + 1) * UNIT] = active.astype(bf16)
    moe = dot(act_s[...], dw[...].reshape(UNITS_DEV * UNIT, D)).astype(bf16)
    for s in range(2):
        for c in range(CHUNKS):
            moe_s[c * DRAFT:(c + 1) * DRAFT, :] = moe[s * DRAFT:(s + 1) * DRAFT, c * CW:(c + 1) * CW]
        msend[s * HALF:(s + 1) * HALF] = (
            dot(permt_s[...], moe_s[...]).astype(bf16).reshape(HALF, ROWS, CW)
        )

    each(N_TP, lambda k: m_copy(k, tp_peer(k), t).start())
    mrecv[t] = msend[t]
    each(4, lambda k: page_copy(k, x).wait_send())
    each(N_REQ, lambda k: q8_copy(k, g).wait_send())
    each(N_REQ, lambda k: r8_copy(k, g).wait_send())
    each(N_TP, lambda k: q_copy(k, t).wait_send())
    each(HALF, lambda k: kv_copy(k, t_in).wait_send())
    each(N_TP, lambda k: o_copy(k, 0, t).wait_send())
    each(N_TP, lambda k: n_copy(k, t).wait_send())
    each(N_TP, lambda k: m_copy(k, 0, tp_peer(k)).wait_recv())
    moe_own = jnp.sum(mrecv[...].astype(f32), axis=0)
    for c in range(CHUNKS):
        flat_s[0:TOK, c * CW:(c + 1) * CW] = moe_own[c * TOK:(c + 1) * TOK, :]
    layer_ref[...] = (hidden + flat_s[0:TOK, :]).astype(bf16)
    each(N_TP, lambda k: m_copy(k, 0, t).wait_send())


def per_device(
    queries, new_kv, residual, placement, lengths, page_table, cache_keys, cache_values,
    parents, accept_leaf, out_weight, norm_gain, router_weight, expert_ids, gate_up, down_weight,
):
    vmem = pl.BlockSpec(memory_space=pltpu.VMEM)
    hbm = pl.BlockSpec(memory_space=pltpu.MemorySpace.HBM)
    dma = pltpu.SemaphoreType.DMA
    return pl.pallas_call(
        kernel,
        out_shape=(
            jax.ShapeDtypeStruct((TOK, D), bf16),
            jax.ShapeDtypeStruct((TOK, D), bf16),
            jax.ShapeDtypeStruct((TOK, 1024), bf16),
        ),
        in_specs=[hbm] * 16,
        out_specs=(vmem, vmem, vmem),
        scratch_shapes=[
            pltpu.VMEM((TOK, D), bf16),
            pltpu.VMEM((TOK, 1024), bf16),
            pltpu.VMEM((TOK, D), bf16),
            pltpu.SMEM((2,), jnp.int32),
            pltpu.SMEM((2,), jnp.int32),
            pltpu.SMEM((2,), jnp.int32),
            pltpu.VMEM((2, PAGE, 512), bf16),
            pltpu.VMEM((2, PAGE, 512), bf16),
            pltpu.VMEM((2, DRAFT), jnp.int32),
            pltpu.SMEM((2,), jnp.int32),
            pltpu.VMEM((D, D), bf16),
            pltpu.VMEM((1, D), f32),
            pltpu.VMEM((EXPERTS, D), bf16),
            pltpu.VMEM((8, GROUP), jnp.int32),
            pltpu.VMEM((UNITS_DEV, D, 2 * UNIT), bf16),
            pltpu.VMEM((UNITS_DEV, UNIT, D), bf16),
            pltpu.VMEM((N_REQ, CHUNKS, ROWS, 128), bf16),
            pltpu.VMEM((N_REQ, ROWS, 640), bf16),
            pltpu.VMEM((CHUNKS, ROWS, 128), bf16),
            pltpu.VMEM((N_TP, ROWS, 128), bf16),
            pltpu.VMEM((HALF, ROWS, 256), bf16),
            pltpu.VMEM((CHUNKS, 4, PAGE, 128), bf16),
            pltpu.VMEM((4, 4, PAGE, 128), bf16),
            pltpu.VMEM((N_TP, ROWS, 256), bf16),
            pltpu.VMEM((N_TP, ROWS, 256), bf16),
            pltpu.VMEM((N_TP, ROWS, CW), bf16),
            pltpu.VMEM((N_TP, ROWS, CW), bf16),
            pltpu.VMEM((N_TP, ROWS, CW), bf16),
            pltpu.VMEM((CHUNKS * ROWS, 128), f32),
            pltpu.VMEM((ROWS, CW), f32),
            pltpu.VMEM((8, D), f32),
            pltpu.VMEM((8, D), f32),
            pltpu.VMEM((256, 256), bf16),
            pltpu.VMEM((256, 256), bf16),
            pltpu.VMEM((GROUP, D), bf16),
            pltpu.VMEM((GROUP, UNITS_DEV * UNIT), bf16),
            pltpu.VMEM((256, CW), bf16),
            dma((16,)),
            dma((4,)), dma((4,)),
            dma((N_REQ,)), dma((N_REQ,)), dma((N_REQ,)), dma((N_REQ,)),
            dma((N_TP,)), dma((N_TP,)), dma((HALF,)), dma((HALF,)),
            dma((N_TP,)), dma((N_TP,)), dma((N_TP,)), dma((N_TP,)), dma((N_TP,)), dma((N_TP,)),
        ],
        compiler_params=pltpu.CompilerParams(
            collective_id=0, has_side_effects=True, vmem_limit_bytes=64 << 20
        ),
        name="verify_layer",
    )(
        queries, new_kv, residual, placement, lengths, page_table.reshape(2),
        cache_keys, cache_values, parents, accept_leaf, out_weight, norm_gain,
        router_weight.T, expert_ids.T, gate_up, down_weight,
    )


def solution(mesh):
    in_specs = (
        P(("req", "tp"), None),
        P(("req", "tp"), None),
        P(("req", "tp"), None),
        P("req"),
        P("req"),
        P("req", None, "tp"),
        P(("req", "tp"), None, None),
        P(("req", "tp"), None, None),
        P("req", None),
        P("req"),
        P(),
        P(),
        P(),
        P("req", None),
        P("tp", None, None),
        P("tp", None, None),
    )
    out_specs = (P(("req", "tp"), None), P(("req", "tp"), None), P(("req", "tp"), None))
    return jax.shard_map(
        per_device, mesh=mesh, in_specs=in_specs, out_specs=out_specs, check_vma=False
    )
```

```python
import functools

import jax
import jax.numpy as jnp
from jax import lax
from jax.experimental import pallas as pl
from jax.experimental.pallas import tpu as pltpu
from jax.sharding import PartitionSpec as P

HEADS = 24
KV_HEADS = 8
HEAD = 64
D = 1536
EXPERTS = 40
FF_E = 512
UNIT = 128
UNITS_DEV = 5
DRAFT = 64
PAGE = 128
N_REQ = 8
N_TP = 32
TOK = 4
CHUNKS = 4
CW = D // CHUNKS
HALF = N_TP // 2
ROWS = CHUNKS * TOK
GROUP = N_TP * TOK
FAR = (3, 5, 4)

neg_big = -1e30
norm_eps = 1e-06
MESH = pl.DeviceIdType.MESH
f32 = jnp.float32
bf16 = jnp.bfloat16


def iota(shape, dim):
    return lax.broadcasted_iota(jnp.int32, shape, dim)


def ones_at(mask):
    return jnp.where(mask, 1.0, 0.0).astype(bf16)


def dot(a, b):
    return jnp.dot(a, b, preferred_element_type=f32)


def dot_t(a, b):
    return lax.dot_general(a, b, (((1,), (1,)), ((), ())), preferred_element_type=f32)


def softmax_block(stacked, keys, values, lo, hi, ones_rhs, valid):
    count = keys.shape[0]
    keys_two = jnp.concatenate([keys * lo, keys * hi], axis=0)
    values_two = jnp.concatenate([values * lo, values * hi], axis=0)
    scores = dot_t(stacked, keys_two)
    s_lo = jnp.where(valid, scores[:, :count], neg_big)
    s_hi = jnp.where(valid, scores[:, count:], neg_big)
    m_lo = jnp.max(s_lo, axis=1, keepdims=True)
    m_hi = jnp.max(s_hi, axis=1, keepdims=True)
    w_lo = jnp.where(valid, jnp.exp(s_lo - m_lo), 0.0).astype(bf16)
    w_hi = jnp.where(valid, jnp.exp(s_hi - m_hi), 0.0).astype(bf16)
    weights = jnp.concatenate([w_lo, w_hi], axis=1)
    both = dot(weights, jnp.concatenate([values_two, ones_rhs], axis=1))
    out, total = both[:, :128], both[:, 128:]
    rows = out.shape[0]
    first = iota((rows, 128), 1) < HEAD
    top = jnp.where(first, m_lo, m_hi)
    some = total > 0.0
    safe = jnp.where(some, total, 1.0)
    return out / safe, jnp.where(some, top + jnp.log(safe), neg_big)


def two_ones(count):
    row = iota((2 * count, 128), 0)
    lane = iota((2 * count, 128), 1)
    return ones_at((row >= count) == (lane >= HEAD))


def kernel(
    q_hbm, kv_hbm, res_hbm, placement_hbm, lengths_hbm, table_hbm, keys_hbm, vals_hbm,
    par_hbm, leaf_hbm, ow_hbm, gain_hbm, rw_hbm, ids_hbm, gu_hbm, dw_hbm,
    attn_ref, layer_ref, acc_ref,
    q_ref, kv_ref, res_ref, placement, lengths, table, kbuf, vbuf,
    par_ref, leaf, ow, gain_ref, rw, ids_ref, gu, dw,
    q8, r8, qown, qall, kvall, pages_send, pages, osend, orecv, nall, msend, mrow, msum, mrecv,
    heads_s, chunk_s, flat_s, res_s, perm_s, permt_s, nfull, act_s, moe_s,
    wsem, sems, far_sems, row_sems,
):
    g = lax.axis_index("req")
    t = lax.axis_index("tp")
    x = t % 4
    z = t // 4
    row_start = t - x
    half = t // HALF
    t_in = t % HALF

    def req_peer(k):
        return lax.rem(g + k, N_REQ)

    def tp_peer(k):
        return lax.rem(t // 4 + k // 4, 8) * 4 + lax.rem(t % 4 + k % 4, 4)

    def slot_peer(k):
        return half * HALF + lax.rem(t_in + k, HALF)

    barrier = pltpu.get_barrier_semaphore()

    def greet_req(k, carry):
        pl.semaphore_signal(barrier, inc=1, device_id={"req": req_peer(k)}, device_id_type=MESH)
        return carry

    def greet_tp(k, carry):
        pl.semaphore_signal(barrier, inc=1, device_id={"tp": tp_peer(k)}, device_id_type=MESH)
        return carry

    def load(i, source, target):
        copy = pltpu.make_async_copy(source, target, wsem.at[i])
        copy.start()
        return copy

    load_q = load(0, q_hbm, q_ref)
    load_kv = load(1, kv_hbm, kv_ref)
    load_res = load(2, res_hbm, res_ref)
    lax.fori_loop(1, N_REQ, greet_req, 0)
    lax.fori_loop(1, N_TP, greet_tp, 0)
    load_placement = load(3, placement_hbm, placement)
    load_par = load(4, par_hbm, par_ref)
    load_leaf = load(5, leaf_hbm, leaf)
    load_lengths = load(6, lengths_hbm, lengths)
    load_table = load(7, table_hbm, table)
    load_keys = load(8, keys_hbm, kbuf)
    load_vals = load(9, vals_hbm, vbuf)
    load_gain = load(10, gain_hbm, gain_ref.at[0])
    load_ids = load(11, ids_hbm, ids_ref)
    load_rw = load(12, rw_hbm, rw)
    load_ow = load(13, ow_hbm, ow)
    load_gu = load(14, gu_hbm, gu)
    load_dw = load(15, dw_hbm, dw)

    load_q.wait()
    q_in = q_ref[...].astype(f32) * (HEAD ** -0.5)
    heads_s[...] = jnp.zeros_like(heads_s)
    for c in range(CHUNKS):
        for r in range(3):
            for k in range(2):
                at = c * CW + (k * 3 + r) * HEAD
                row = c * ROWS + r * TOK
                heads_s[row:row + TOK, k * HEAD:(k + 1) * HEAD] = q_in[:, at:at + HEAD]
    q8[g] = heads_s[...].astype(bf16).reshape(CHUNKS, ROWS, 128)
    def page_copy(k, source):
        peer = lax.rem(x + k, 4)
        return pltpu.make_async_remote_copy(
            src_ref=pages_send.at[peer], dst_ref=pages.at[source], send_sem=sems.at[0],
            recv_sem=sems.at[1], device_id={"tp": row_start + peer}, device_id_type=MESH,
        )

    def q8_copy(k, source):
        return pltpu.make_async_remote_copy(
            src_ref=q8.at[source], dst_ref=q8.at[source], send_sem=sems.at[2],
            recv_sem=sems.at[3], device_id={"req": req_peer(k)}, device_id_type=MESH,
        )

    def r8_copy(k, source):
        return pltpu.make_async_remote_copy(
            src_ref=r8.at[source], dst_ref=r8.at[source], send_sem=sems.at[4],
            recv_sem=sems.at[5], device_id={"req": req_peer(k)}, device_id_type=MESH,
        )

    def q_copy(k, source):
        return pltpu.make_async_remote_copy(
            src_ref=qown.at[lax.rem(x + k % 4, 4)], dst_ref=qall.at[source], send_sem=sems.at[6],
            recv_sem=sems.at[7], device_id={"tp": tp_peer(k)}, device_id_type=MESH,
        )

    def kv_copy(k, source):
        return pltpu.make_async_remote_copy(
            src_ref=kvall.at[source], dst_ref=kvall.at[source], send_sem=sems.at[8],
            recv_sem=sems.at[9], device_id={"tp": slot_peer(k)}, device_id_type=MESH,
        )

    def o_copy(k, block, source):
        return pltpu.make_async_remote_copy(
            src_ref=osend.at[block], dst_ref=orecv.at[source], send_sem=sems.at[10],
            recv_sem=sems.at[11], device_id={"tp": tp_peer(k)}, device_id_type=MESH,
        )

    def far_copy(k):
        block = t
        return pltpu.make_async_remote_copy(
            src_ref=nall.at[block], dst_ref=nall.at[block], send_sem=sems.at[12],
            recv_sem=far_sems.at[k], device_id={"tp": lax.rem(z + k, 8) * 4 + x}, device_id_type=MESH,
        )

    def n_copy(block, peer):
        return pltpu.make_async_remote_copy(
            src_ref=nall.at[block], dst_ref=nall.at[block], send_sem=sems.at[12],
            recv_sem=sems.at[13], device_id={"tp": peer}, device_id_type=MESH,
        )

    def row_copy(zone, k):
        peer = lax.rem(x + k, 4)
        return pltpu.make_async_remote_copy(
            src_ref=msend.at[zone * 4 + peer], dst_ref=mrow.at[zone * 4 + x], send_sem=sems.at[14],
            recv_sem=row_sems.at[zone], device_id={"tp": row_start + peer}, device_id_type=MESH,
        )

    def zone_copy(zone):
        return pltpu.make_async_remote_copy(
            src_ref=msum.at[zone], dst_ref=mrecv.at[z], send_sem=sems.at[15],
            recv_sem=sems.at[16], device_id={"tp": zone * 4 + x}, device_id_type=MESH,
        )

    def near_start(k):
        zone = k // 4
        far = functools.reduce(jnp.logical_or, [zone == f for f in FAR])

        @pl.when(jnp.logical_not(far))
        def _():
            n_copy(t, tp_peer(k)).start()

    def await_bytes(refs, index):
        pltpu.make_async_copy(refs, refs, sems.at[index]).wait()

    def each(count, step):
        def body(k, carry):
            step(k)
            return carry

        lax.fori_loop(1, count, body, 0)

    pl.semaphore_wait(barrier, N_REQ - 1 + N_TP - 1)

    each(N_REQ, lambda k: q8_copy(k, g).start())
    load_kv.wait()
    kv_in = kv_ref[...].astype(f32)
    for c in range(CHUNKS):
        chunk_s[c * TOK:(c + 1) * TOK, 0:128] = kv_in[:, c * 128:(c + 1) * 128]
        chunk_s[c * TOK:(c + 1) * TOK, 128:256] = kv_in[:, 512 + c * 128:512 + (c + 1) * 128]
    r8[g, :, 0:256] = chunk_s[:, 0:256].astype(bf16)
    load_res.wait()
    res_in = res_ref[...].astype(f32)
    for c in range(CHUNKS):
        chunk_s[c * TOK:(c + 1) * TOK, :] = res_in[:, c * CW:(c + 1) * CW]
    r8[g, :, 256:640] = chunk_s[...].astype(bf16)

    each(N_REQ, lambda k: r8_copy(k, g).start())

    load_table.wait()
    load_keys.wait()
    load_vals.wait()
    for s in range(2):
        page_k = kbuf[table[s]]
        page_v = vbuf[table[s]]
        for c in range(CHUNKS):
            pages_send[c, s] = page_k[:, c * 128:(c + 1) * 128]
            pages_send[c, 2 + s] = page_v[:, c * 128:(c + 1) * 128]
    each(4, lambda k: page_copy(k, x).start())
    pages[x] = pages_send[x]

    row_a = iota((256, 256), 0)
    row_b = iota((256, 256), 1)
    perm_s[...] = ones_at(
        row_b == ((row_a & 63) >> 2) * ROWS + (row_a >> 6) * TOK + (row_a & 3)
    )
    permt_s[...] = ones_at(
        row_a == ((row_b & 63) >> 2) * ROWS + (row_b >> 6) * TOK + (row_b & 3)
    )

    node_m = iota((DRAFT, DRAFT), 0)
    node_n = iota((DRAFT, DRAFT), 1)
    load_par.wait()
    load_leaf.wait()
    parent_row = par_ref[pl.ds(half, 1), :]
    reach_t = ones_at(((node_m == parent_row) & (node_n > 0)) | (node_m == node_n))
    for _ in range(6):
        reach_t = jnp.minimum(dot(reach_t, reach_t), 1.0).astype(bf16)
    own_node = t_in * TOK + (iota((ROWS, DRAFT), 0) & 3)
    lane_node = iota((ROWS, DRAFT), 1)
    tree_node = t_in * TOK + (iota((CHUNKS * ROWS, DRAFT), 0) & 3)
    tree_lane = iota((CHUNKS * ROWS, DRAFT), 1)
    spread_row = iota((DRAFT, 256), 0)
    spread_lane = iota((DRAFT, 256), 1)
    spread = ones_at(spread_row == (spread_lane >> 4) * TOK + (spread_lane & 3))
    same_chunk = ((iota((ROWS, 256), 1) >> 2) & 3) == (iota((ROWS, 256), 0) >> 2)
    tree_chunk = ((iota((CHUNKS * ROWS, 256), 1) >> 2) & 3) == (iota((CHUNKS * ROWS, 256), 0) >> 4)
    own_reach = dot_t(ones_at(tree_lane == tree_node), reach_t).astype(bf16)
    tree_valid = jnp.where(tree_chunk, dot(own_reach, spread), 0.0) > 0.5
    flags = dot_t(ones_at(lane_node == leaf[half]), reach_t)
    rank = dot(flags.astype(bf16), ones_at(node_m <= node_n)) - 1.0
    chosen = ones_at((flags > 0.5) & (rank == own_node.astype(f32)))
    choice = jnp.where(same_chunk, dot(chosen, spread), 0.0).astype(bf16)

    lane_one = iota((1, 128), 1)
    lo = ones_at(lane_one < HEAD)
    hi = ones_at(lane_one >= HEAD)

    await_bytes(q8.at[0:N_REQ - 1], 3)
    load_placement.wait()
    source_group = lax.shift_right_logical(placement[half], 1)
    own_q = q8[source_group]
    qown[...] = own_q
    qall[t] = qown[x]
    each(N_TP, lambda k: q_copy(k, t).start())
    await_bytes(r8.at[0:N_REQ - 1], 5)
    own_kvres = r8[source_group]
    kvall[t_in] = own_kvres[:, 0:256]
    each(HALF, lambda k: kv_copy(k, t_in).start())
    own_res = own_kvres[:, 256:640].astype(f32)
    for c in range(CHUNKS):
        res_s[0:TOK, c * CW:(c + 1) * CW] = own_res[c * TOK:(c + 1) * TOK, :]

    span = 4 * PAGE
    ones_page = two_ones(span)
    stat_lane = iota((256, 128), 1) & (HEAD - 1)
    load_lengths.wait()
    await_bytes(pages.at[0:3], 1)
    await_bytes(qall.at[0:N_TP - 1], 7)
    for s in range(2):
        valid = row_start * PAGE + iota((1, span), 1) < lengths[s]
        out, lse = softmax_block(
            qall[s * HALF:(s + 1) * HALF].reshape(256, 128), pages[:, s].reshape(span, 128),
            pages[:, 2 + s].reshape(span, 128), lo, hi, ones_page, valid,
        )
        first = lse.astype(bf16).astype(f32)
        rest = lse - first
        second = rest.astype(bf16).astype(f32)
        stats = jnp.where(stat_lane == 0, first, jnp.where(stat_lane == 1, second, rest - second))
        osend[s * HALF:(s + 1) * HALF, :, 0:128] = out.astype(bf16).reshape(HALF, ROWS, 128)
        osend[s * HALF:(s + 1) * HALF, :, 128:256] = stats.astype(bf16).reshape(HALF, ROWS, 128)

    each(N_TP, lambda k: o_copy(k, tp_peer(k), t).start())
    orecv[t] = osend[t]

    await_bytes(kvall.at[0:HALF - 1], 9)
    kv_slot = kvall[...].reshape(256, 256)
    accepted = dot(choice, kv_slot)
    for c in range(CHUNKS):
        acc_ref[:, c * 128:(c + 1) * 128] = accepted[c * TOK:(c + 1) * TOK, 0:128].astype(bf16)
        acc_ref[:, 512 + c * 128:512 + (c + 1) * 128] = (
            accepted[c * TOK:(c + 1) * TOK, 128:256].astype(bf16)
        )
    tree_out, tree_lse = softmax_block(
        own_q.reshape(CHUNKS * ROWS, 128), kv_slot[:, 0:128], kv_slot[:, 128:256], lo, hi,
        two_ones(256), tree_valid,
    )
    ex_row = iota((128, 128), 0)
    expand = ones_at(((ex_row >> 6) == (iota((128, 128), 1) >> 6)) & ((ex_row & (HEAD - 1)) < 3))

    await_bytes(orecv.at[0:N_TP - 1], 11)
    lse_all = dot(orecv[:, :, 128:256].reshape(N_TP * ROWS, 128), expand)
    lse_all = lse_all.reshape(N_TP // 4, CHUNKS * ROWS, 128)
    out_all = orecv[:, :, 0:128].reshape(N_TP // 4, CHUNKS * ROWS, 128).astype(f32)
    top = jnp.maximum(jnp.max(lse_all, axis=0), tree_lse)
    scale = jnp.exp(lse_all - top[None])
    tree_scale = jnp.exp(tree_lse - top)
    total = jnp.sum(scale, axis=0) + tree_scale
    joined = (jnp.sum(scale * out_all, axis=0) + tree_scale * tree_out) / total
    for c in range(CHUNKS):
        for r in range(3):
            for k in range(2):
                at = c * CW + (k * 3 + r) * HEAD
                row = c * ROWS + r * TOK
                flat_s[0:TOK, at:at + HEAD] = joined[row:row + TOK, k * HEAD:(k + 1) * HEAD]
    attn = flat_s[0:TOK, :].astype(bf16)
    attn_ref[...] = attn

    load_ow.wait()
    load_gain.wait()
    hidden = res_s[0:TOK, :] + dot(attn, ow[...])
    mean = jnp.mean(hidden * hidden, axis=-1, keepdims=True)
    normed = (hidden * lax.rsqrt(mean + norm_eps) * gain_ref[...]).astype(bf16).astype(f32)
    for c in range(CHUNKS):
        chunk_s[c * TOK:(c + 1) * TOK, :] = normed[:, c * CW:(c + 1) * CW]
    nall[t] = chunk_s[...].astype(bf16)

    for k in FAR:
        far_copy(k).start()
    each(N_TP, lambda k: near_start(k))
    expert_row = iota((EXPERTS, GROUP), 0)
    load_ids.wait()
    ids = ids_ref[...]
    picked = expert_row == ids[0:1]
    for k in range(1, ids.shape[0]):
        picked = picked | (expert_row == ids[k:k + 1])
    for k in FAR:
        far_copy(k).wait_recv()
        block = lax.rem(z + 8 - k, 8) * 4 + x
        for i in range(1, 4):
            n_copy(block, row_start + lax.rem(x + i, 4)).start()
    load_rw.wait()
    load_gu.wait()
    load_dw.wait()
    await_bytes(nall.at[0:N_TP - 1 - len(FAR)], 13)
    for s in range(2):
        rows = dot(perm_s[...], nall[s * HALF:(s + 1) * HALF].reshape(256, CW)).astype(bf16)
        for c in range(CHUNKS):
            nfull[s * DRAFT:(s + 1) * DRAFT, c * CW:(c + 1) * CW] = rows[c * DRAFT:(c + 1) * DRAFT]
    normed_all = nfull[...]
    expo = jnp.where(picked, jnp.exp(dot_t(rw[...], normed_all)), 0.0)
    routing = expo / jnp.sum(expo, axis=0, keepdims=True)
    first_expert = t * UNITS_DEV // (FF_E // UNIT)
    two = jnp.concatenate(
        [
            jnp.sum(jnp.where(expert_row == first_expert + k, routing, 0.0), axis=0, keepdims=True)
            for k in range(2)
        ]
        + [jnp.zeros((GROUP - 2, GROUP), f32)],
        axis=0,
    )
    columns = jnp.transpose(two)
    for u in range(UNITS_DEV):
        same = (t * UNITS_DEV + u) // (FF_E // UNIT) == first_expert
        share = jnp.where(same, columns[:, 0:1], columns[:, 1:2])
        both = dot(normed_all, gu[u])
        gate = both[:, :UNIT]
        active = gate / (1.0 + jnp.exp(-gate)) * both[:, UNIT:] * share
        act_s[:, u * UNIT:(u + 1) * UNIT] = active.astype(bf16)
    moe = dot(act_s[...], dw[...].reshape(UNITS_DEV * UNIT, D)).astype(bf16)
    for s in range(2):
        for c in range(CHUNKS):
            moe_s[c * DRAFT:(c + 1) * DRAFT, :] = moe[s * DRAFT:(s + 1) * DRAFT, c * CW:(c + 1) * CW]
        msend[s * HALF:(s + 1) * HALF] = (
            dot(permt_s[...], moe_s[...]).astype(bf16).reshape(HALF, ROWS, CW)
        )

    zones = [lax.rem(z + k, 8) for k in (4, 3, 5, 2, 6, 1, 7, 0)]
    for zone in zones:
        for k in (1, 3, 2):
            row_copy(zone, k).start()
    await_bytes(pages_send.at[0:3], 0)
    await_bytes(q8.at[0:N_REQ - 1], 2)
    await_bytes(r8.at[0:N_REQ - 1], 4)
    await_bytes(qall.at[0:N_TP - 1], 6)
    await_bytes(kvall.at[0:HALF - 1], 8)
    await_bytes(osend.at[0:N_TP - 1], 10)
    await_bytes(nall.at[0:N_TP - 1], 12)
    for i, zone in enumerate(zones):
        pltpu.make_async_copy(mrow.at[0:3], mrow.at[0:3], row_sems.at[zone]).wait()
        part = msend[zone * 4 + x].astype(f32)
        for k in range(1, 4):
            part = part + mrow[zone * 4 + lax.rem(x + k, 4)].astype(f32)
        if i < 7:
            msum[zone] = part.astype(bf16)
            zone_copy(zone).start()
        else:
            moe_own = part
    await_bytes(mrecv.at[0:7], 16)
    for zone in zones[:7]:
        moe_own = moe_own + mrecv[zone].astype(f32)
    for c in range(CHUNKS):
        flat_s[0:TOK, c * CW:(c + 1) * CW] = moe_own[c * TOK:(c + 1) * TOK, :]
    layer_ref[...] = (hidden + flat_s[0:TOK, :]).astype(bf16)
    await_bytes(msend.at[0:24], 14)
    await_bytes(msum.at[0:7], 15)


def hand_out(attn_in, layer_in, acc_in, attn_out, layer_out, acc_out, sems):
    copies = [
        pltpu.make_async_copy(a, b, sems.at[i])
        for i, (a, b) in enumerate([(attn_in, attn_out), (layer_in, layer_out), (acc_in, acc_out)])
    ]
    for copy in copies:
        copy.start()
    for copy in copies:
        copy.wait()


def per_device(
    queries, new_kv, residual, placement, lengths, page_table, cache_keys, cache_values,
    parents, accept_leaf, out_weight, norm_gain, router_weight, expert_ids, gate_up, down_weight,
):
    vmem = pl.BlockSpec(memory_space=pltpu.VMEM)
    hbm = pl.BlockSpec(memory_space=pltpu.MemorySpace.HBM)
    dma = pltpu.SemaphoreType.DMA
    shapes = (
        jax.ShapeDtypeStruct((TOK, D), bf16),
        jax.ShapeDtypeStruct((TOK, D), bf16),
        jax.ShapeDtypeStruct((TOK, 1024), bf16),
    )
    results = pl.pallas_call(
        kernel,
        out_shape=shapes,
        in_specs=[hbm] * 16,
        out_specs=(vmem, vmem, vmem),
        scratch_shapes=[
            pltpu.VMEM((TOK, D), bf16),
            pltpu.VMEM((TOK, 1024), bf16),
            pltpu.VMEM((TOK, D), bf16),
            pltpu.SMEM((2,), jnp.int32),
            pltpu.SMEM((2,), jnp.int32),
            pltpu.SMEM((2,), jnp.int32),
            pltpu.VMEM((2, PAGE, 512), bf16),
            pltpu.VMEM((2, PAGE, 512), bf16),
            pltpu.VMEM((2, DRAFT), jnp.int32),
            pltpu.SMEM((2,), jnp.int32),
            pltpu.VMEM((D, D), bf16),
            pltpu.VMEM((1, D), f32),
            pltpu.VMEM((EXPERTS, D), bf16),
            pltpu.VMEM((8, GROUP), jnp.int32),
            pltpu.VMEM((UNITS_DEV, D, 2 * UNIT), bf16),
            pltpu.VMEM((UNITS_DEV, UNIT, D), bf16),
            pltpu.VMEM((N_REQ, CHUNKS, ROWS, 128), bf16),
            pltpu.VMEM((N_REQ, ROWS, 640), bf16),
            pltpu.VMEM((CHUNKS, ROWS, 128), bf16),
            pltpu.VMEM((N_TP, ROWS, 128), bf16),
            pltpu.VMEM((HALF, ROWS, 256), bf16),
            pltpu.VMEM((CHUNKS, 4, PAGE, 128), bf16),
            pltpu.VMEM((4, 4, PAGE, 128), bf16),
            pltpu.VMEM((N_TP, ROWS, 256), bf16),
            pltpu.VMEM((N_TP, ROWS, 256), bf16),
            pltpu.VMEM((N_TP, ROWS, CW), bf16),
            pltpu.VMEM((N_TP, ROWS, CW), bf16),
            pltpu.VMEM((N_TP, ROWS, CW), bf16),
            pltpu.VMEM((8, ROWS, CW), bf16),
            pltpu.VMEM((8, ROWS, CW), bf16),
            pltpu.VMEM((CHUNKS * ROWS, 128), f32),
            pltpu.VMEM((ROWS, CW), f32),
            pltpu.VMEM((8, D), f32),
            pltpu.VMEM((8, D), f32),
            pltpu.VMEM((256, 256), bf16),
            pltpu.VMEM((256, 256), bf16),
            pltpu.VMEM((GROUP, D), bf16),
            pltpu.VMEM((GROUP, UNITS_DEV * UNIT), bf16),
            pltpu.VMEM((256, CW), bf16),
            dma((16,)),
            dma((17,)), dma((8,)), dma((8,)),
        ],
        compiler_params=pltpu.CompilerParams(
            collective_id=0, has_side_effects=True, vmem_limit_bytes=64 << 20
        ),
        name="verify_layer",
    )(
        queries, new_kv, residual, placement, lengths, page_table.reshape(2),
        cache_keys, cache_values, parents, accept_leaf, out_weight, norm_gain,
        router_weight.T, expert_ids.T, gate_up, down_weight,
    )
    return pl.pallas_call(
        hand_out,
        out_shape=shapes,
        in_specs=[hbm] * 3,
        out_specs=(hbm, hbm, hbm),
        scratch_shapes=[dma((3,))],
        compiler_params=pltpu.CompilerParams(vmem_limit_bytes=64 << 20),
        name="hand_out",
    )(*results)


def solution(mesh):
    in_specs = (
        P(("req", "tp"), None),
        P(("req", "tp"), None),
        P(("req", "tp"), None),
        P("req"),
        P("req"),
        P("req", None, "tp"),
        P(("req", "tp"), None, None),
        P(("req", "tp"), None, None),
        P("req", None),
        P("req"),
        P(),
        P(),
        P(),
        P("req", None),
        P("tp", None, None),
        P("tp", None, None),
    )
    out_specs = (P(("req", "tp"), None), P(("req", "tp"), None), P(("req", "tp"), None))
    return jax.shard_map(
        per_device, mesh=mesh, in_specs=in_specs, out_specs=out_specs, check_vma=False
    )
```

```python
import functools

import jax
import jax.numpy as jnp
from jax import lax
from jax.experimental import pallas as pl
from jax.experimental.pallas import tpu as pltpu
from jax.sharding import PartitionSpec as P

HEADS = 24
KV_HEADS = 8
HEAD = 64
D = 1536
EXPERTS = 40
FF_E = 512
UNIT = 128
UNITS_DEV = 5
DRAFT = 64
PAGE = 128
N_REQ = 8
N_TP = 32
TOK = 4
CHUNKS = 4
CW = D // CHUNKS
HALF = N_TP // 2
ROWS = CHUNKS * TOK
GROUP = N_TP * TOK
FAR = (3, 5, 4)

neg_big = -1e30
norm_eps = 1e-06
MESH = pl.DeviceIdType.MESH
f32 = jnp.float32
bf16 = jnp.bfloat16


def iota(shape, dim):
    return lax.broadcasted_iota(jnp.int32, shape, dim)


def ones_at(mask):
    return jnp.where(mask, 1.0, 0.0).astype(bf16)


def dot(a, b):
    return jnp.dot(a, b, preferred_element_type=f32)


def dot_t(a, b):
    return lax.dot_general(a, b, (((1,), (1,)), ((), ())), preferred_element_type=f32)


def two_heads(block, lo, hi):
    return jnp.concatenate([block * lo, block * hi], axis=0)


def softmax_block(stacked, keys_two, values_two, valid):
    count = keys_two.shape[0] // 2
    scores = dot_t(stacked, keys_two)
    s_lo = jnp.where(valid, scores[:, :count], neg_big)
    s_hi = jnp.where(valid, scores[:, count:], neg_big)
    m_lo = jnp.max(s_lo, axis=1, keepdims=True)
    m_hi = jnp.max(s_hi, axis=1, keepdims=True)
    w_lo = jnp.where(valid, jnp.exp(s_lo - m_lo), 0.0).astype(bf16)
    w_hi = jnp.where(valid, jnp.exp(s_hi - m_hi), 0.0).astype(bf16)
    both = dot(jnp.concatenate([w_lo, w_hi], axis=1), values_two)
    out, total = both[:, :128], both[:, 128:]
    first = iota((out.shape[0], 128), 1) < HEAD
    top = jnp.where(first, m_lo, m_hi)
    some = total > 0.0
    safe = jnp.where(some, total, 1.0)
    return out / safe, jnp.where(some, top + jnp.log(safe), neg_big)


def two_ones(count):
    row = iota((2 * count, 128), 0)
    lane = iota((2 * count, 128), 1)
    return ones_at((row >= count) == (lane >= HEAD))


def kernel(
    q_hbm, kv_hbm, res_hbm, placement_hbm, lengths_hbm, table_hbm, keys_hbm, vals_hbm,
    par_hbm, leaf_hbm, ow_hbm, gain_hbm, rw_hbm, ids_hbm, gu_hbm, dw_hbm,
    attn_ref, layer_ref, acc_ref,
    placement, lengths, table, kbuf, vbuf,
    par_ref, leaf, ow, gain_ref, rw, ids_ref, gu, dw,
    q8, kv8, res8, qown, qall, kvall, pages_send, pages, osend, orecv, nall, msend, mrow, msum, mrecv,
    heads_s, chunk_s, flat_s, perm_s, permt_s, lift_s, kz_s, vz_s, nfull, act_s, moe_s,
    wsem, sems, far_sems, row_sems,
):
    g = lax.axis_index("req")
    t = lax.axis_index("tp")
    x = t % 4
    z = t // 4
    row_start = t - x
    half = t // HALF
    t_in = t % HALF

    def req_peer(k):
        return lax.rem(g + k, N_REQ)

    def offset(k):
        i, j = (k - 1) // 4, (k - 1) % 4
        along_z = 4 + (1 - 2 * (i % 2)) * ((i + 1) // 2)
        return along_z, 2 + (1 - 2 * (j % 2)) * ((j + 1) // 2)

    def tp_peer(k):
        along_z, along_x = offset(k)
        return lax.rem(z + along_z, 8) * 4 + lax.rem(x + along_x, 4)

    def slot_peer(k):
        return half * HALF + lax.rem(t_in + k, HALF)

    barrier = pltpu.get_barrier_semaphore()

    def greet_req(k, carry):
        pl.semaphore_signal(barrier, inc=1, device_id={"req": req_peer(k)}, device_id_type=MESH)
        return carry

    def greet_tp(k, carry):
        pl.semaphore_signal(barrier, inc=1, device_id={"tp": tp_peer(k)}, device_id_type=MESH)
        return carry

    def load(i, source, target):
        copy = pltpu.make_async_copy(source, target, wsem.at[i])
        copy.start()
        return copy

    lax.fori_loop(1, N_REQ, greet_req, 0)
    lax.fori_loop(1, N_TP, greet_tp, 0)
    load_q = load(0, q_hbm, q8.at[g])
    load_kv = load(1, kv_hbm, kv8.at[g])
    load_res = load(2, res_hbm, res8.at[g])
    load_placement = load(3, placement_hbm, placement)
    load_par = load(4, par_hbm, par_ref)
    load_leaf = load(5, leaf_hbm, leaf)
    load_lengths = load(6, lengths_hbm, lengths)
    load_table = load(7, table_hbm, table)
    load_keys = load(8, keys_hbm, kbuf)
    load_vals = load(9, vals_hbm, vbuf)
    load_gain = load(10, gain_hbm, gain_ref.at[0])
    load_ids = load(11, ids_hbm, ids_ref)
    load_rw = load(12, rw_hbm, rw)
    load_ow = load(13, ow_hbm, ow)
    load_gu = load(14, gu_hbm, gu)
    load_dw = load(15, dw_hbm, dw)

    def page_copy(k, source):
        peer = lax.rem(x + k, 4)
        return pltpu.make_async_remote_copy(
            src_ref=pages_send.at[peer], dst_ref=pages.at[source], send_sem=sems.at[0],
            recv_sem=sems.at[1], device_id={"tp": row_start + peer}, device_id_type=MESH,
        )

    def q8_copy(k, source):
        return pltpu.make_async_remote_copy(
            src_ref=q_hbm, dst_ref=q8.at[source], send_sem=sems.at[2],
            recv_sem=sems.at[3], device_id={"req": req_peer(k)}, device_id_type=MESH,
        )

    def kv8_copy(k, source):
        return pltpu.make_async_remote_copy(
            src_ref=kv_hbm, dst_ref=kv8.at[source], send_sem=sems.at[4],
            recv_sem=sems.at[5], device_id={"req": req_peer(k)}, device_id_type=MESH,
        )

    def res8_copy(k, source):
        return pltpu.make_async_remote_copy(
            src_ref=res_hbm, dst_ref=res8.at[source], send_sem=sems.at[17],
            recv_sem=sems.at[18], device_id={"req": req_peer(k)}, device_id_type=MESH,
        )

    def q_copy(k, source):
        return pltpu.make_async_remote_copy(
            src_ref=qown.at[lax.rem(x + offset(k)[1], 4)], dst_ref=qall.at[source], send_sem=sems.at[6],
            recv_sem=sems.at[7], device_id={"tp": tp_peer(k)}, device_id_type=MESH,
        )

    def kv_copy(k, source):
        return pltpu.make_async_remote_copy(
            src_ref=kvall.at[source], dst_ref=kvall.at[source], send_sem=sems.at[8],
            recv_sem=sems.at[9], device_id={"tp": slot_peer(k)}, device_id_type=MESH,
        )

    def o_copy(k, block, source):
        return pltpu.make_async_remote_copy(
            src_ref=osend.at[block], dst_ref=orecv.at[source], send_sem=sems.at[10],
            recv_sem=sems.at[11], device_id={"tp": tp_peer(k)}, device_id_type=MESH,
        )

    def far_copy(k):
        block = t
        return pltpu.make_async_remote_copy(
            src_ref=nall.at[block], dst_ref=nall.at[block], send_sem=sems.at[12],
            recv_sem=far_sems.at[k], device_id={"tp": lax.rem(z + k, 8) * 4 + x}, device_id_type=MESH,
        )

    def n_copy(block, peer):
        return pltpu.make_async_remote_copy(
            src_ref=nall.at[block], dst_ref=nall.at[block], send_sem=sems.at[12],
            recv_sem=sems.at[13], device_id={"tp": peer}, device_id_type=MESH,
        )

    def row_copy(zone, k):
        peer = lax.rem(x + k, 4)
        return pltpu.make_async_remote_copy(
            src_ref=msend.at[zone * 4 + peer], dst_ref=mrow.at[zone * 4 + x], send_sem=sems.at[14],
            recv_sem=row_sems.at[zone], device_id={"tp": row_start + peer}, device_id_type=MESH,
        )

    def zone_copy(zone):
        return pltpu.make_async_remote_copy(
            src_ref=msum.at[zone], dst_ref=mrecv.at[z], send_sem=sems.at[15],
            recv_sem=sems.at[16], device_id={"tp": zone * 4 + x}, device_id_type=MESH,
        )

    def near_start(k):
        zone = offset(k)[0]
        far = functools.reduce(jnp.logical_or, [zone == f for f in FAR])

        @pl.when(jnp.logical_not(far))
        def _():
            n_copy(t, tp_peer(k)).start()

    def await_bytes(refs, index):
        pltpu.make_async_copy(refs, refs, sems.at[index]).wait()

    def each(count, step):
        def body(k, carry):
            step(k)
            return carry

        lax.fori_loop(1, count, body, 0)

    pl.semaphore_wait(barrier, N_REQ - 1 + N_TP - 1)

    each(N_REQ, lambda k: q8_copy(k, g).start())
    each(N_REQ, lambda k: kv8_copy(k, g).start())
    each(N_REQ, lambda k: res8_copy(k, g).start())

    load_table.wait()
    load_keys.wait()
    load_vals.wait()
    for s in range(2):
        page_k = kbuf[table[s]]
        page_v = vbuf[table[s]]
        for c in range(CHUNKS):
            pages_send[c, s] = page_k[:, c * 128:(c + 1) * 128]
            pages_send[c, 2 + s] = page_v[:, c * 128:(c + 1) * 128]
    each(4, lambda k: page_copy(k, x).start())
    pages[x] = pages_send[x]
    lane_one = iota((1, 128), 1)
    lo = ones_at(lane_one < HEAD)
    hi = ones_at(lane_one >= HEAD)

    load_q.wait()
    load_placement.wait()
    source_group = lax.shift_right_logical(placement[half], 1)
    heads_s[...] = jnp.zeros_like(heads_s)
    await_bytes(q8.at[0:N_REQ - 1], 3)
    q_in = q8[source_group].astype(f32) * (HEAD ** -0.5)
    for c in range(CHUNKS):
        for r in range(3):
            for k in range(2):
                at = c * CW + (k * 3 + r) * HEAD
                row = c * ROWS + r * TOK
                heads_s[row:row + TOK, k * HEAD:(k + 1) * HEAD] = q_in[:, at:at + HEAD]
    own_q = heads_s[...].astype(bf16).reshape(CHUNKS, ROWS, 128)
    qown[...] = own_q
    qall[t] = qown[x]
    each(N_TP, lambda k: q_copy(k, t).start())
    load_kv.wait()
    await_bytes(kv8.at[0:N_REQ - 1], 5)
    kv_in = kv8[source_group].astype(f32)
    for c in range(CHUNKS):
        chunk_s[c * TOK:(c + 1) * TOK, 0:128] = kv_in[:, c * 128:(c + 1) * 128]
        chunk_s[c * TOK:(c + 1) * TOK, 128:256] = kv_in[:, 512 + c * 128:512 + (c + 1) * 128]
    kvall[t_in] = chunk_s[:, 0:256].astype(bf16)
    each(HALF, lambda k: kv_copy(k, t_in).start())
    load_res.wait()
    await_bytes(res8.at[0:N_REQ - 1], 18)
    own_res = res8[source_group].astype(f32)

    row_a = iota((256, 256), 0)
    row_b = iota((256, 256), 1)
    perm_s[...] = ones_at(
        row_b == ((row_a & 63) >> 2) * ROWS + (row_a >> 6) * TOK + (row_a & 3)
    )
    permt_s[...] = ones_at(
        row_a == ((row_b & 63) >> 2) * ROWS + (row_b >> 6) * TOK + (row_b & 3)
    )

    lift_r = iota((256, 768), 0)
    lift_c = iota((256, 768), 1)
    lift_s[...] = ones_at(
        ((lift_r >> 4) == ((lift_c & 255) >> 4)) & ((lift_r & 15) == 3 * TOK + (lift_c >> 8))
    )
    span = 4 * PAGE
    ones_page = two_ones(span)
    block_row = iota((256, 128), 0) & (ROWS - 1)
    block_lane = iota((256, 128), 1)
    diag = (block_lane & (HEAD - 1)) == block_row
    load_lengths.wait()
    await_bytes(pages.at[0:3], 1)
    for s in range(2):
        kz_s[s] = two_heads(pages[:, s].reshape(span, 128), lo, hi)
        vz_s[s, :, 0:128] = two_heads(pages[:, 2 + s].reshape(span, 128), lo, hi)
        vz_s[s, :, 128:256] = ones_page
    await_bytes(qall.at[0:N_TP - 1], 7)
    for s in range(2):
        valid = row_start * PAGE + iota((1, span), 1) < lengths[s]
        out, lse = softmax_block(
            qall[s * HALF:(s + 1) * HALF].reshape(256, 128), kz_s[s], vz_s[s], valid
        )
        first = lse.astype(bf16).astype(f32)
        rest = lse - first
        second = rest.astype(bf16).astype(f32)
        parts = [jnp.where(diag, part, 0.0).astype(bf16) for part in (first, second, rest - second)]
        lifted = dot(lift_s[...], jnp.concatenate(parts, axis=0))
        osend[s * HALF:(s + 1) * HALF] = (
            jnp.where(block_row < 3 * TOK, out, lifted).astype(bf16).reshape(HALF, ROWS, 128)
        )

    each(N_TP, lambda k: o_copy(k, tp_peer(k), t).start())
    orecv[t] = osend[t]

    node_m = iota((DRAFT, DRAFT), 0)
    node_n = iota((DRAFT, DRAFT), 1)
    load_par.wait()
    load_leaf.wait()
    parent_row = par_ref[pl.ds(half, 1), :]
    reach_t = ones_at(((node_m == parent_row) & (node_n > 0)) | (node_m == node_n))
    for _ in range(6):
        reach_t = jnp.minimum(dot(reach_t, reach_t), 1.0).astype(bf16)
    own_node = t_in * TOK + (iota((ROWS, DRAFT), 0) & 3)
    lane_node = iota((ROWS, DRAFT), 1)
    tree_node = t_in * TOK + (iota((CHUNKS * ROWS, DRAFT), 0) & 3)
    tree_lane = iota((CHUNKS * ROWS, DRAFT), 1)
    spread_row = iota((DRAFT, 256), 0)
    spread_lane = iota((DRAFT, 256), 1)
    spread = ones_at(spread_row == (spread_lane >> 4) * TOK + (spread_lane & 3))
    same_chunk = ((iota((ROWS, 256), 1) >> 2) & 3) == (iota((ROWS, 256), 0) >> 2)
    tree_chunk = ((iota((CHUNKS * ROWS, 256), 1) >> 2) & 3) == (iota((CHUNKS * ROWS, 256), 0) >> 4)
    own_reach = dot_t(ones_at(tree_lane == tree_node), reach_t).astype(bf16)
    tree_valid = jnp.where(tree_chunk, dot(own_reach, spread), 0.0) > 0.5
    flags = dot_t(ones_at(lane_node == leaf[half]), reach_t)
    rank = dot(flags.astype(bf16), ones_at(node_m <= node_n)) - 1.0
    chosen = ones_at((flags > 0.5) & (rank == own_node.astype(f32)))
    choice = jnp.where(same_chunk, dot(chosen, spread), 0.0).astype(bf16)
    await_bytes(kvall.at[0:HALF - 1], 9)
    kv_slot = kvall[...].reshape(256, 256)
    accepted = dot(choice, kv_slot)
    for c in range(CHUNKS):
        acc_ref[:, c * 128:(c + 1) * 128] = accepted[c * TOK:(c + 1) * TOK, 0:128].astype(bf16)
        acc_ref[:, 512 + c * 128:512 + (c + 1) * 128] = (
            accepted[c * TOK:(c + 1) * TOK, 128:256].astype(bf16)
        )
    tree_out, tree_lse = softmax_block(
        own_q.reshape(CHUNKS * ROWS, 128), two_heads(kv_slot[:, 0:128], lo, hi),
        jnp.concatenate([two_heads(kv_slot[:, 128:256], lo, hi), two_ones(256)], axis=1), tree_valid,
    )
    drop = ones_at(
        ((row_a >> 4) == (row_b >> 4)) & ((row_b & 15) >= 3 * TOK) & ((row_b & 15) < 3 * TOK + 3)
    )

    await_bytes(orecv.at[0:N_TP - 1], 11)
    lse_parts = []
    for s in range(2):
        packed = orecv[s * HALF:(s + 1) * HALF].reshape(256, 128)
        own_lane = jnp.where(diag, dot(drop, packed), 0.0)
        lse_lo = jnp.sum(jnp.where(block_lane < HEAD, own_lane, 0.0), axis=1, keepdims=True)
        lse_hi = jnp.sum(jnp.where(block_lane < HEAD, 0.0, own_lane), axis=1, keepdims=True)
        lse_parts.append(jnp.where(block_lane < HEAD, lse_lo, lse_hi))
    lse_all = jnp.concatenate(lse_parts, axis=0).reshape(N_TP // 4, CHUNKS * ROWS, 128)
    out_all = orecv[...].reshape(N_TP // 4, CHUNKS * ROWS, 128).astype(f32)
    top = jnp.maximum(jnp.max(lse_all, axis=0), tree_lse)
    scale = jnp.exp(lse_all - top[None])
    tree_scale = jnp.exp(tree_lse - top)
    total = jnp.sum(scale, axis=0) + tree_scale
    joined = (jnp.sum(scale * out_all, axis=0) + tree_scale * tree_out) / total
    for c in range(CHUNKS):
        for r in range(3):
            for k in range(2):
                at = c * CW + (k * 3 + r) * HEAD
                row = c * ROWS + r * TOK
                flat_s[0:TOK, at:at + HEAD] = joined[row:row + TOK, k * HEAD:(k + 1) * HEAD]
    attn = flat_s[0:TOK, :].astype(bf16)
    attn_ref[...] = attn

    load_ow.wait()
    load_gain.wait()
    hidden = own_res + dot(attn, ow[...])
    mean = jnp.mean(hidden * hidden, axis=-1, keepdims=True)
    normed = (hidden * lax.rsqrt(mean + norm_eps) * gain_ref[...]).astype(bf16).astype(f32)
    for c in range(CHUNKS):
        chunk_s[c * TOK:(c + 1) * TOK, :] = normed[:, c * CW:(c + 1) * CW]
    nall[t] = chunk_s[...].astype(bf16)

    for k in FAR:
        far_copy(k).start()
    each(N_TP, lambda k: near_start(k))
    expert_row = iota((EXPERTS, GROUP), 0)
    load_ids.wait()
    ids = ids_ref[...]
    picked = expert_row == ids[0:1]
    for k in range(1, ids.shape[0]):
        picked = picked | (expert_row == ids[k:k + 1])
    for k in FAR:
        far_copy(k).wait_recv()
        block = lax.rem(z + 8 - k, 8) * 4 + x
        for i in range(1, 4):
            n_copy(block, row_start + lax.rem(x + i, 4)).start()
    load_rw.wait()
    load_gu.wait()
    load_dw.wait()
    await_bytes(nall.at[0:N_TP - 1 - len(FAR)], 13)
    for s in range(2):
        rows = dot(perm_s[...], nall[s * HALF:(s + 1) * HALF].reshape(256, CW)).astype(bf16)
        for c in range(CHUNKS):
            nfull[s * DRAFT:(s + 1) * DRAFT, c * CW:(c + 1) * CW] = rows[c * DRAFT:(c + 1) * DRAFT]
    normed_all = nfull[...]
    expo = jnp.where(picked, jnp.exp(dot_t(rw[...], normed_all)), 0.0)
    routing = expo / jnp.sum(expo, axis=0, keepdims=True)
    first_expert = t * UNITS_DEV // (FF_E // UNIT)
    two = jnp.concatenate(
        [
            jnp.sum(jnp.where(expert_row == first_expert + k, routing, 0.0), axis=0, keepdims=True)
            for k in range(2)
        ]
        + [jnp.zeros((GROUP - 2, GROUP), f32)],
        axis=0,
    )
    columns = jnp.transpose(two)
    for u in range(UNITS_DEV):
        same = (t * UNITS_DEV + u) // (FF_E // UNIT) == first_expert
        share = jnp.where(same, columns[:, 0:1], columns[:, 1:2])
        both = dot(normed_all, gu[u])
        gate = both[:, :UNIT]
        active = gate / (1.0 + jnp.exp(-gate)) * both[:, UNIT:] * share
        act_s[:, u * UNIT:(u + 1) * UNIT] = active.astype(bf16)
    moe = dot(act_s[...], dw[...].reshape(UNITS_DEV * UNIT, D)).astype(bf16)
    for s in range(2):
        for c in range(CHUNKS):
            moe_s[c * DRAFT:(c + 1) * DRAFT, :] = moe[s * DRAFT:(s + 1) * DRAFT, c * CW:(c + 1) * CW]
        msend[s * HALF:(s + 1) * HALF] = (
            dot(permt_s[...], moe_s[...]).astype(bf16).reshape(HALF, ROWS, CW)
        )

    zones = [lax.rem(z + k, 8) for k in (4, 3, 5, 2, 6, 1, 7, 0)]
    for zone in zones:
        for k in (2, 1, 3):
            row_copy(zone, k).start()
    await_bytes(pages_send.at[0:3], 0)
    await_bytes(q8.at[0:N_REQ - 1], 2)
    await_bytes(kv8.at[0:N_REQ - 1], 4)
    await_bytes(res8.at[0:N_REQ - 1], 17)
    await_bytes(qall.at[0:N_TP - 1], 6)
    await_bytes(kvall.at[0:HALF - 1], 8)
    await_bytes(osend.at[0:N_TP - 1], 10)
    await_bytes(nall.at[0:N_TP - 1], 12)
    for i, zone in enumerate(zones):
        pltpu.make_async_copy(mrow.at[0:3], mrow.at[0:3], row_sems.at[zone]).wait()
        part = msend[zone * 4 + x].astype(f32)
        for k in range(1, 4):
            part = part + mrow[zone * 4 + lax.rem(x + k, 4)].astype(f32)
        if i < 7:
            msum[zone] = part.astype(bf16)
            zone_copy(zone).start()
        else:
            moe_own = part
    await_bytes(mrecv.at[0:7], 16)
    for zone in zones[:7]:
        moe_own = moe_own + mrecv[zone].astype(f32)
    for c in range(CHUNKS):
        flat_s[0:TOK, c * CW:(c + 1) * CW] = moe_own[c * TOK:(c + 1) * TOK, :]
    layer_ref[...] = (hidden + flat_s[0:TOK, :]).astype(bf16)
    await_bytes(msend.at[0:24], 14)
    await_bytes(msum.at[0:7], 15)


def hand_out(attn_in, layer_in, acc_in, attn_out, layer_out, acc_out):
    attn_out[...] = attn_in[...]
    layer_out[...] = layer_in[...]
    acc_out[...] = acc_in[...]


def per_device(
    queries, new_kv, residual, placement, lengths, page_table, cache_keys, cache_values,
    parents, accept_leaf, out_weight, norm_gain, router_weight, expert_ids, gate_up, down_weight,
):
    vmem = pl.BlockSpec(memory_space=pltpu.VMEM)
    hbm = pl.BlockSpec(memory_space=pltpu.MemorySpace.HBM)
    dma = pltpu.SemaphoreType.DMA
    shapes = (
        jax.ShapeDtypeStruct((TOK, D), bf16),
        jax.ShapeDtypeStruct((TOK, D), bf16),
        jax.ShapeDtypeStruct((TOK, 1024), bf16),
    )
    results = pl.pallas_call(
        kernel,
        out_shape=shapes,
        in_specs=[hbm] * 16,
        out_specs=(vmem, vmem, vmem),
        scratch_shapes=[
            pltpu.SMEM((2,), jnp.int32),
            pltpu.SMEM((2,), jnp.int32),
            pltpu.SMEM((2,), jnp.int32),
            pltpu.VMEM((2, PAGE, 512), bf16),
            pltpu.VMEM((2, PAGE, 512), bf16),
            pltpu.VMEM((2, DRAFT), jnp.int32),
            pltpu.SMEM((2,), jnp.int32),
            pltpu.VMEM((D, D), bf16),
            pltpu.VMEM((1, D), f32),
            pltpu.VMEM((EXPERTS, D), bf16),
            pltpu.VMEM((8, GROUP), jnp.int32),
            pltpu.VMEM((UNITS_DEV, D, 2 * UNIT), bf16),
            pltpu.VMEM((UNITS_DEV, UNIT, D), bf16),
            pltpu.VMEM((N_REQ, TOK, D), bf16),
            pltpu.VMEM((N_REQ, TOK, 1024), bf16),
            pltpu.VMEM((N_REQ, TOK, D), bf16),
            pltpu.VMEM((CHUNKS, ROWS, 128), bf16),
            pltpu.VMEM((N_TP, ROWS, 128), bf16),
            pltpu.VMEM((HALF, ROWS, 256), bf16),
            pltpu.VMEM((CHUNKS, 4, PAGE, 128), bf16),
            pltpu.VMEM((4, 4, PAGE, 128), bf16),
            pltpu.VMEM((N_TP, ROWS, 128), bf16),
            pltpu.VMEM((N_TP, ROWS, 128), bf16),
            pltpu.VMEM((N_TP, ROWS, CW), bf16),
            pltpu.VMEM((N_TP, ROWS, CW), bf16),
            pltpu.VMEM((N_TP, ROWS, CW), bf16),
            pltpu.VMEM((8, ROWS, CW), bf16),
            pltpu.VMEM((8, ROWS, CW), bf16),
            pltpu.VMEM((CHUNKS * ROWS, 128), f32),
            pltpu.VMEM((ROWS, CW), f32),
            pltpu.VMEM((8, D), f32),
            pltpu.VMEM((256, 256), bf16),
            pltpu.VMEM((256, 256), bf16),
            pltpu.VMEM((256, 768), bf16),
            pltpu.VMEM((2, 8 * PAGE, 128), bf16),
            pltpu.VMEM((2, 8 * PAGE, 256), bf16),
            pltpu.VMEM((GROUP, D), bf16),
            pltpu.VMEM((GROUP, UNITS_DEV * UNIT), bf16),
            pltpu.VMEM((256, CW), bf16),
            dma((16,)),
            dma((19,)), dma((8,)), dma((8,)),
        ],
        compiler_params=pltpu.CompilerParams(
            collective_id=0, has_side_effects=True, vmem_limit_bytes=64 << 20
        ),
        name="verify_layer",
    )(
        queries, new_kv, residual, placement, lengths, page_table.reshape(2),
        cache_keys, cache_values, parents, accept_leaf, out_weight, norm_gain,
        router_weight.T, expert_ids.T, gate_up, down_weight,
    )
    return pl.pallas_call(
        hand_out,
        out_shape=shapes,
        in_specs=[vmem] * 3,
        out_specs=(vmem, vmem, vmem),
        compiler_params=pltpu.CompilerParams(vmem_limit_bytes=64 << 20),
        name="hand_out",
    )(*results)


def solution(mesh):
    in_specs = (
        P(("req", "tp"), None),
        P(("req", "tp"), None),
        P(("req", "tp"), None),
        P("req"),
        P("req"),
        P("req", None, "tp"),
        P(("req", "tp"), None, None),
        P(("req", "tp"), None, None),
        P("req", None),
        P("req"),
        P(),
        P(),
        P(),
        P("req", None),
        P("tp", None, None),
        P("tp", None, None),
    )
    out_specs = (P(("req", "tp"), None), P(("req", "tp"), None), P(("req", "tp"), None))
    return jax.shard_map(
        per_device, mesh=mesh, in_specs=in_specs, out_specs=out_specs, check_vma=False
    )
```

```python
import functools

import jax
import jax.numpy as jnp
from jax import lax
from jax.experimental import pallas as pl
from jax.experimental.pallas import tpu as pltpu
from jax.sharding import PartitionSpec as P

HEADS = 24
KV_HEADS = 8
HEAD = 64
D = 1536
EXPERTS = 40
FF_E = 512
UNIT = 128
UNITS_DEV = 5
DRAFT = 64
PAGE = 128
N_REQ = 8
N_TP = 32
TOK = 4
CHUNKS = 4
CW = D // CHUNKS
HALF = N_TP // 2
ROWS = CHUNKS * TOK
GROUP = N_TP * TOK
FAR = (2, 6, 3, 5, 4)

neg_big = -1e30
norm_eps = 1e-06
MESH = pl.DeviceIdType.MESH
f32 = jnp.float32
bf16 = jnp.bfloat16


def iota(shape, dim):
    return lax.broadcasted_iota(jnp.int32, shape, dim)


def ones_at(mask):
    return jnp.where(mask, 1.0, 0.0).astype(bf16)


def dot(a, b):
    return jnp.dot(a, b, preferred_element_type=f32)


def dot_t(a, b):
    return lax.dot_general(a, b, (((1,), (1,)), ((), ())), preferred_element_type=f32)


def two_heads(block, lo, hi):
    return jnp.concatenate([block * lo, block * hi], axis=0)


def softmax_block(stacked, keys_two, values_two, valid):
    count = keys_two.shape[0] // 2
    scores = dot_t(stacked, keys_two)
    s_lo = jnp.where(valid, scores[:, :count], neg_big)
    s_hi = jnp.where(valid, scores[:, count:], neg_big)
    m_lo = jnp.max(s_lo, axis=1, keepdims=True)
    m_hi = jnp.max(s_hi, axis=1, keepdims=True)
    w_lo = jnp.where(valid, jnp.exp(s_lo - m_lo), 0.0).astype(bf16)
    w_hi = jnp.where(valid, jnp.exp(s_hi - m_hi), 0.0).astype(bf16)
    both = dot(jnp.concatenate([w_lo, w_hi], axis=1), values_two)
    out, total = both[:, :128], both[:, 128:]
    first = iota((out.shape[0], 128), 1) < HEAD
    top = jnp.where(first, m_lo, m_hi)
    some = total > 0.0
    safe = jnp.where(some, total, 1.0)
    return out / safe, jnp.where(some, top + jnp.log(safe), neg_big)


def two_ones(count):
    row = iota((2 * count, 128), 0)
    lane = iota((2 * count, 128), 1)
    return ones_at((row >= count) == (lane >= HEAD))


def kernel(
    q_hbm, kv_hbm, res_hbm, placement_hbm, lengths_hbm, table_hbm, keys_hbm, vals_hbm,
    par_hbm, leaf_hbm, ow_hbm, gain_hbm, rw_hbm, ids_hbm, gu_hbm, dw_hbm,
    attn_ref, layer_ref, acc_ref,
    placement, lengths, table, kbuf, vbuf,
    par_ref, leaf, ow, gain_ref, rw, ids_ref, gu, dw,
    q8, kv8, res8, qown, qall, kvall, pages_send, pages, osend, orecv, nall, msend, mrow, msum, mnear, mrecv,
    heads_s, chunk_s, flat_s, perm_s, permt_s, lift_s, kz_s, vz_s, nfull, act_s, moe_s,
    wsem, sems, far_sems, row_sems,
):
    g = lax.axis_index("req")
    t = lax.axis_index("tp")
    x = t % 4
    z = t // 4
    row_start = t - x
    half = t // HALF
    t_in = t % HALF

    def req_peer(k):
        return lax.rem(g + k, N_REQ)

    def offset(k):
        i, j = (k - 1) // 4, (k - 1) % 4
        along_z = 4 + (1 - 2 * (i % 2)) * ((i + 1) // 2)
        return along_z, 2 + (1 - 2 * (j % 2)) * ((j + 1) // 2)

    def tp_peer(k):
        along_z, along_x = offset(k)
        return lax.rem(z + along_z, 8) * 4 + lax.rem(x + along_x, 4)

    def slot_peer(k):
        return half * HALF + lax.rem(t_in + k, HALF)

    barrier = pltpu.get_barrier_semaphore()

    def greet_req(k, carry):
        pl.semaphore_signal(barrier, inc=1, device_id={"req": req_peer(k)}, device_id_type=MESH)
        return carry

    def greet_tp(k, carry):
        pl.semaphore_signal(barrier, inc=1, device_id={"tp": tp_peer(k)}, device_id_type=MESH)
        return carry

    def load(i, source, target):
        copy = pltpu.make_async_copy(source, target, wsem.at[i])
        copy.start()
        return copy

    lax.fori_loop(1, N_REQ, greet_req, 0)
    lax.fori_loop(1, N_TP, greet_tp, 0)
    load_q = load(0, q_hbm, q8.at[g])
    load_kv = load(1, kv_hbm, kv8.at[g])
    load_res = load(2, res_hbm, res8.at[g])
    load_placement = load(3, placement_hbm, placement)
    load_par = load(4, par_hbm, par_ref)
    load_leaf = load(5, leaf_hbm, leaf)
    load_lengths = load(6, lengths_hbm, lengths)
    load_table = load(7, table_hbm, table)
    load_keys = load(8, keys_hbm, kbuf)
    load_vals = load(9, vals_hbm, vbuf)
    load_gain = load(10, gain_hbm, gain_ref.at[0])
    load_ids = load(11, ids_hbm, ids_ref)
    load_rw = load(12, rw_hbm, rw)
    load_ow = load(13, ow_hbm, ow)
    load_gu = load(14, gu_hbm, gu)
    load_dw = load(15, dw_hbm, dw)

    def page_copy(k, source):
        peer = lax.rem(x + k, 4)
        return pltpu.make_async_remote_copy(
            src_ref=pages_send.at[peer], dst_ref=pages.at[source], send_sem=sems.at[0],
            recv_sem=sems.at[1], device_id={"tp": row_start + peer}, device_id_type=MESH,
        )

    def q8_copy(k, source):
        return pltpu.make_async_remote_copy(
            src_ref=q_hbm, dst_ref=q8.at[source], send_sem=sems.at[2],
            recv_sem=sems.at[3], device_id={"req": req_peer(k)}, device_id_type=MESH,
        )

    def kv8_copy(k, source):
        return pltpu.make_async_remote_copy(
            src_ref=kv_hbm, dst_ref=kv8.at[source], send_sem=sems.at[4],
            recv_sem=sems.at[5], device_id={"req": req_peer(k)}, device_id_type=MESH,
        )

    def res8_copy(k, source):
        return pltpu.make_async_remote_copy(
            src_ref=res_hbm, dst_ref=res8.at[source], send_sem=sems.at[17],
            recv_sem=sems.at[18], device_id={"req": req_peer(k)}, device_id_type=MESH,
        )

    def q_copy(k, source):
        return pltpu.make_async_remote_copy(
            src_ref=qown.at[lax.rem(x + offset(k)[1], 4)], dst_ref=qall.at[source], send_sem=sems.at[6],
            recv_sem=sems.at[19], device_id={"tp": tp_peer(k)}, device_id_type=MESH,
        )

    def kv_copy(k, source):
        return pltpu.make_async_remote_copy(
            src_ref=kvall.at[source], dst_ref=kvall.at[source], send_sem=sems.at[8],
            recv_sem=sems.at[9], device_id={"tp": slot_peer(k)}, device_id_type=MESH,
        )

    def o_copy(k, block, source):
        return pltpu.make_async_remote_copy(
            src_ref=osend.at[block], dst_ref=orecv.at[source], send_sem=sems.at[10],
            recv_sem=sems.at[11], device_id={"tp": tp_peer(k)}, device_id_type=MESH,
        )

    def far_copy(k):
        block = t
        return pltpu.make_async_remote_copy(
            src_ref=nall.at[block], dst_ref=nall.at[block], send_sem=sems.at[12],
            recv_sem=far_sems.at[k], device_id={"tp": lax.rem(z + k, 8) * 4 + x}, device_id_type=MESH,
        )

    def n_copy(block, peer):
        return pltpu.make_async_remote_copy(
            src_ref=nall.at[block], dst_ref=nall.at[block], send_sem=sems.at[12],
            recv_sem=sems.at[13], device_id={"tp": peer}, device_id_type=MESH,
        )

    def row_copy(zone, k):
        peer = lax.rem(x + k, 4)
        return pltpu.make_async_remote_copy(
            src_ref=msend.at[zone * 4 + peer], dst_ref=mrow.at[zone * 4 + x], send_sem=sems.at[14],
            recv_sem=row_sems.at[zone], device_id={"tp": row_start + peer}, device_id_type=MESH,
        )

    def zone_copy(zone):
        return pltpu.make_async_remote_copy(
            src_ref=msum.at[zone], dst_ref=mrecv.at[z], send_sem=sems.at[15],
            recv_sem=sems.at[16], device_id={"tp": zone * 4 + x}, device_id_type=MESH,
        )

    def near_start(k):
        zone = offset(k)[0]
        far = functools.reduce(jnp.logical_or, [zone == f for f in FAR])

        @pl.when(jnp.logical_not(far))
        def _():
            n_copy(t, tp_peer(k)).start()

    def direct_copy(along_z, k):
        peer = lax.rem(z + along_z, 8) * 4 + lax.rem(x + k, 4)
        return pltpu.make_async_remote_copy(
            src_ref=msend.at[peer], dst_ref=mnear.at[t], send_sem=sems.at[14],
            recv_sem=sems.at[7], device_id={"tp": peer}, device_id_type=MESH,
        )

    def await_bytes(refs, index):
        pltpu.make_async_copy(refs, refs, sems.at[index]).wait()

    def each(count, step):
        def body(k, carry):
            step(k)
            return carry

        lax.fori_loop(1, count, body, 0)

    pl.semaphore_wait(barrier, N_REQ - 1 + N_TP - 1)

    each(N_REQ, lambda k: q8_copy(k, g).start())
    each(N_REQ, lambda k: kv8_copy(k, g).start())
    each(N_REQ, lambda k: res8_copy(k, g).start())

    load_table.wait()
    load_keys.wait()
    load_vals.wait()
    for s in range(2):
        page_k = kbuf[table[s]]
        page_v = vbuf[table[s]]
        for c in range(CHUNKS):
            pages_send[c, s] = page_k[:, c * 128:(c + 1) * 128]
            pages_send[c, 2 + s] = page_v[:, c * 128:(c + 1) * 128]
    each(4, lambda k: page_copy(k, x).start())
    pages[x] = pages_send[x]
    lane_one = iota((1, 128), 1)
    lo = ones_at(lane_one < HEAD)
    hi = ones_at(lane_one >= HEAD)

    load_q.wait()
    load_placement.wait()
    source_group = lax.shift_right_logical(placement[half], 1)
    heads_s[...] = jnp.zeros_like(heads_s)
    await_bytes(q8.at[0:N_REQ - 1], 3)
    q_in = q8[source_group].astype(f32) * (HEAD ** -0.5)
    for c in range(CHUNKS):
        for r in range(3):
            for k in range(2):
                at = c * CW + (k * 3 + r) * HEAD
                row = c * ROWS + r * TOK
                heads_s[row:row + TOK, k * HEAD:(k + 1) * HEAD] = q_in[:, at:at + HEAD]
    own_q = heads_s[...].astype(bf16).reshape(CHUNKS, ROWS, 128)
    qown[...] = own_q
    qall[t] = qown[x]
    each(N_TP, lambda k: q_copy(k, t).start())
    load_kv.wait()
    await_bytes(kv8.at[0:N_REQ - 1], 5)
    kv_in = kv8[source_group].astype(f32)
    for c in range(CHUNKS):
        chunk_s[c * TOK:(c + 1) * TOK, 0:128] = kv_in[:, c * 128:(c + 1) * 128]
        chunk_s[c * TOK:(c + 1) * TOK, 128:256] = kv_in[:, 512 + c * 128:512 + (c + 1) * 128]
    kvall[t_in] = chunk_s[:, 0:256].astype(bf16)
    each(HALF, lambda k: kv_copy(k, t_in).start())
    load_res.wait()
    await_bytes(res8.at[0:N_REQ - 1], 18)
    own_res = res8[source_group].astype(f32)

    row_a = iota((256, 256), 0)
    row_b = iota((256, 256), 1)
    perm_s[...] = ones_at(
        row_b == ((row_a & 63) >> 2) * ROWS + (row_a >> 6) * TOK + (row_a & 3)
    )
    permt_s[...] = ones_at(
        row_a == ((row_b & 63) >> 2) * ROWS + (row_b >> 6) * TOK + (row_b & 3)
    )

    lift_r = iota((256, 768), 0)
    lift_c = iota((256, 768), 1)
    lift_s[...] = ones_at(
        ((lift_r >> 4) == ((lift_c & 255) >> 4)) & ((lift_r & 15) == 3 * TOK + (lift_c >> 8))
    )
    span = 4 * PAGE
    ones_page = two_ones(span)
    block_row = iota((256, 128), 0) & (ROWS - 1)
    block_lane = iota((256, 128), 1)
    diag = (block_lane & (HEAD - 1)) == block_row
    load_lengths.wait()
    await_bytes(pages.at[0:3], 1)
    for s in range(2):
        kz_s[s] = two_heads(pages[:, s].reshape(span, 128), lo, hi)
        vz_s[s, :, 0:128] = two_heads(pages[:, 2 + s].reshape(span, 128), lo, hi)
        vz_s[s, :, 128:256] = ones_page
    await_bytes(qall.at[0:N_TP - 1], 19)
    for s in range(2):
        valid = row_start * PAGE + iota((1, span), 1) < lengths[s]
        out, lse = softmax_block(
            qall[s * HALF:(s + 1) * HALF].reshape(256, 128), kz_s[s], vz_s[s], valid
        )
        first = lse.astype(bf16).astype(f32)
        rest = lse - first
        second = rest.astype(bf16).astype(f32)
        parts = [jnp.where(diag, part, 0.0).astype(bf16) for part in (first, second, rest - second)]
        lifted = dot(lift_s[...], jnp.concatenate(parts, axis=0))
        osend[s * HALF:(s + 1) * HALF] = (
            jnp.where(block_row < 3 * TOK, out, lifted).astype(bf16).reshape(HALF, ROWS, 128)
        )

    each(N_TP, lambda k: o_copy(k, tp_peer(k), t).start())
    orecv[t] = osend[t]

    node_m = iota((DRAFT, DRAFT), 0)
    node_n = iota((DRAFT, DRAFT), 1)
    load_par.wait()
    load_leaf.wait()
    parent_row = par_ref[pl.ds(half, 1), :]
    reach_t = ones_at(((node_m == parent_row) & (node_n > 0)) | (node_m == node_n))
    for _ in range(6):
        reach_t = jnp.minimum(dot(reach_t, reach_t), 1.0).astype(bf16)
    own_node = t_in * TOK + (iota((ROWS, DRAFT), 0) & 3)
    lane_node = iota((ROWS, DRAFT), 1)
    tree_node = t_in * TOK + (iota((CHUNKS * ROWS, DRAFT), 0) & 3)
    tree_lane = iota((CHUNKS * ROWS, DRAFT), 1)
    spread_row = iota((DRAFT, 256), 0)
    spread_lane = iota((DRAFT, 256), 1)
    spread = ones_at(spread_row == (spread_lane >> 4) * TOK + (spread_lane & 3))
    same_chunk = ((iota((ROWS, 256), 1) >> 2) & 3) == (iota((ROWS, 256), 0) >> 2)
    tree_chunk = ((iota((CHUNKS * ROWS, 256), 1) >> 2) & 3) == (iota((CHUNKS * ROWS, 256), 0) >> 4)
    own_reach = dot_t(ones_at(tree_lane == tree_node), reach_t).astype(bf16)
    tree_valid = jnp.where(tree_chunk, dot(own_reach, spread), 0.0) > 0.5
    flags = dot_t(ones_at(lane_node == leaf[half]), reach_t)
    rank = dot(flags.astype(bf16), ones_at(node_m <= node_n)) - 1.0
    chosen = ones_at((flags > 0.5) & (rank == own_node.astype(f32)))
    choice = jnp.where(same_chunk, dot(chosen, spread), 0.0).astype(bf16)
    await_bytes(kvall.at[0:HALF - 1], 9)
    kv_slot = kvall[...].reshape(256, 256)
    accepted = dot(choice, kv_slot)
    for c in range(CHUNKS):
        acc_ref[:, c * 128:(c + 1) * 128] = accepted[c * TOK:(c + 1) * TOK, 0:128].astype(bf16)
        acc_ref[:, 512 + c * 128:512 + (c + 1) * 128] = (
            accepted[c * TOK:(c + 1) * TOK, 128:256].astype(bf16)
        )
    tree_out, tree_lse = softmax_block(
        own_q.reshape(CHUNKS * ROWS, 128), two_heads(kv_slot[:, 0:128], lo, hi),
        jnp.concatenate([two_heads(kv_slot[:, 128:256], lo, hi), two_ones(256)], axis=1), tree_valid,
    )
    drop = ones_at(
        ((row_a >> 4) == (row_b >> 4)) & ((row_b & 15) >= 3 * TOK) & ((row_b & 15) < 3 * TOK + 3)
    )

    await_bytes(orecv.at[0:N_TP - 1], 11)
    lse_parts = []
    for s in range(2):
        packed = orecv[s * HALF:(s + 1) * HALF].reshape(256, 128)
        own_lane = jnp.where(diag, dot(drop, packed), 0.0)
        lse_lo = jnp.sum(jnp.where(block_lane < HEAD, own_lane, 0.0), axis=1, keepdims=True)
        lse_hi = jnp.sum(jnp.where(block_lane < HEAD, 0.0, own_lane), axis=1, keepdims=True)
        lse_parts.append(jnp.where(block_lane < HEAD, lse_lo, lse_hi))
    lse_all = jnp.concatenate(lse_parts, axis=0).reshape(N_TP // 4, CHUNKS * ROWS, 128)
    out_all = orecv[...].reshape(N_TP // 4, CHUNKS * ROWS, 128).astype(f32)
    top = jnp.maximum(jnp.max(lse_all, axis=0), tree_lse)
    scale = jnp.exp(lse_all - top[None])
    tree_scale = jnp.exp(tree_lse - top)
    total = jnp.sum(scale, axis=0) + tree_scale
    joined = (jnp.sum(scale * out_all, axis=0) + tree_scale * tree_out) / total
    for c in range(CHUNKS):
        for r in range(3):
            for k in range(2):
                at = c * CW + (k * 3 + r) * HEAD
                row = c * ROWS + r * TOK
                flat_s[0:TOK, at:at + HEAD] = joined[row:row + TOK, k * HEAD:(k + 1) * HEAD]
    attn = flat_s[0:TOK, :].astype(bf16)
    attn_ref[...] = attn

    load_ow.wait()
    load_gain.wait()
    hidden = own_res + dot(attn, ow[...])
    mean = jnp.mean(hidden * hidden, axis=-1, keepdims=True)
    normed = (hidden * lax.rsqrt(mean + norm_eps) * gain_ref[...]).astype(bf16).astype(f32)
    for c in range(CHUNKS):
        chunk_s[c * TOK:(c + 1) * TOK, :] = normed[:, c * CW:(c + 1) * CW]
    nall[t] = chunk_s[...].astype(bf16)

    for k in FAR:
        far_copy(k).start()
    each(N_TP, lambda k: near_start(k))
    expert_row = iota((EXPERTS, GROUP), 0)
    load_ids.wait()
    ids = ids_ref[...]
    picked = expert_row == ids[0:1]
    for k in range(1, ids.shape[0]):
        picked = picked | (expert_row == ids[k:k + 1])
    for k in FAR:
        far_copy(k).wait_recv()
        block = lax.rem(z + 8 - k, 8) * 4 + x
        for i in range(1, 4):
            n_copy(block, row_start + lax.rem(x + i, 4)).start()
    load_rw.wait()
    load_gu.wait()
    load_dw.wait()
    await_bytes(nall.at[0:N_TP - 1 - len(FAR)], 13)
    for s in range(2):
        rows = dot(perm_s[...], nall[s * HALF:(s + 1) * HALF].reshape(256, CW)).astype(bf16)
        for c in range(CHUNKS):
            nfull[s * DRAFT:(s + 1) * DRAFT, c * CW:(c + 1) * CW] = rows[c * DRAFT:(c + 1) * DRAFT]
    normed_all = nfull[...]
    expo = jnp.where(picked, jnp.exp(dot_t(rw[...], normed_all)), 0.0)
    routing = expo / jnp.sum(expo, axis=0, keepdims=True)
    first_expert = t * UNITS_DEV // (FF_E // UNIT)
    two = jnp.concatenate(
        [
            jnp.sum(jnp.where(expert_row == first_expert + k, routing, 0.0), axis=0, keepdims=True)
            for k in range(2)
        ]
        + [jnp.zeros((GROUP - 2, GROUP), f32)],
        axis=0,
    )
    columns = jnp.transpose(two)
    for u in range(UNITS_DEV):
        same = (t * UNITS_DEV + u) // (FF_E // UNIT) == first_expert
        share = jnp.where(same, columns[:, 0:1], columns[:, 1:2])
        both = dot(normed_all, gu[u])
        gate = both[:, :UNIT]
        active = gate / (1.0 + jnp.exp(-gate)) * both[:, UNIT:] * share
        act_s[:, u * UNIT:(u + 1) * UNIT] = active.astype(bf16)
    moe = dot(act_s[...], dw[...].reshape(UNITS_DEV * UNIT, D)).astype(bf16)
    for s in range(2):
        for c in range(CHUNKS):
            moe_s[c * DRAFT:(c + 1) * DRAFT, :] = moe[s * DRAFT:(s + 1) * DRAFT, c * CW:(c + 1) * CW]
        msend[s * HALF:(s + 1) * HALF] = (
            dot(permt_s[...], moe_s[...]).astype(bf16).reshape(HALF, ROWS, CW)
        )

    zones = [lax.rem(z + k, 8) for k in (4, 3, 5)]
    for zone in zones:
        for k in (2, 1, 3):
            row_copy(zone, k).start()
    for along_z in (2, 6, 1, 7):
        for k in (2, 1, 3, 0):
            direct_copy(along_z, k).start()
    for k in (2, 1, 3):
        direct_copy(0, k).start()
    await_bytes(pages_send.at[0:3], 0)
    await_bytes(q8.at[0:N_REQ - 1], 2)
    await_bytes(kv8.at[0:N_REQ - 1], 4)
    await_bytes(res8.at[0:N_REQ - 1], 17)
    await_bytes(qall.at[0:N_TP - 1], 6)
    await_bytes(kvall.at[0:HALF - 1], 8)
    await_bytes(osend.at[0:N_TP - 1], 10)
    await_bytes(nall.at[0:N_TP - 1], 12)
    for i, zone in enumerate(zones):
        pltpu.make_async_copy(mrow.at[0:3], mrow.at[0:3], row_sems.at[zone]).wait()
        part = msend[zone * 4 + x].astype(f32)
        for k in range(1, 4):
            part = part + mrow[zone * 4 + lax.rem(x + k, 4)].astype(f32)
        msum[zone] = part.astype(bf16)
        zone_copy(zone).start()
    moe_own = msend[t].astype(f32)
    await_bytes(mnear.at[0:19], 7)
    for along_z in (2, 6, 1, 7):
        for k in range(4):
            moe_own = moe_own + mnear[lax.rem(z + along_z, 8) * 4 + lax.rem(x + k, 4)].astype(f32)
    for k in range(1, 4):
        moe_own = moe_own + mnear[z * 4 + lax.rem(x + k, 4)].astype(f32)
    await_bytes(mrecv.at[0:3], 16)
    for zone in zones:
        moe_own = moe_own + mrecv[zone].astype(f32)
    for c in range(CHUNKS):
        flat_s[0:TOK, c * CW:(c + 1) * CW] = moe_own[c * TOK:(c + 1) * TOK, :]
    layer_ref[...] = (hidden + flat_s[0:TOK, :]).astype(bf16)
    await_bytes(msend.at[0:28], 14)
    await_bytes(msum.at[0:3], 15)


def hand_out(attn_in, layer_in, acc_in, attn_out, layer_out, acc_out):
    attn_out[...] = attn_in[...]
    layer_out[...] = layer_in[...]
    acc_out[...] = acc_in[...]


def per_device(
    queries, new_kv, residual, placement, lengths, page_table, cache_keys, cache_values,
    parents, accept_leaf, out_weight, norm_gain, router_weight, expert_ids, gate_up, down_weight,
):
    vmem = pl.BlockSpec(memory_space=pltpu.VMEM)
    hbm = pl.BlockSpec(memory_space=pltpu.MemorySpace.HBM)
    dma = pltpu.SemaphoreType.DMA
    shapes = (
        jax.ShapeDtypeStruct((TOK, D), bf16),
        jax.ShapeDtypeStruct((TOK, D), bf16),
        jax.ShapeDtypeStruct((TOK, 1024), bf16),
    )
    results = pl.pallas_call(
        kernel,
        out_shape=tuple(pltpu.VMEM(a.shape, a.dtype) for a in shapes),
        in_specs=[hbm] * 16,
        out_specs=(vmem, vmem, vmem),
        scratch_shapes=[
            pltpu.SMEM((2,), jnp.int32),
            pltpu.SMEM((2,), jnp.int32),
            pltpu.SMEM((2,), jnp.int32),
            pltpu.VMEM((2, PAGE, 512), bf16),
            pltpu.VMEM((2, PAGE, 512), bf16),
            pltpu.VMEM((2, DRAFT), jnp.int32),
            pltpu.SMEM((2,), jnp.int32),
            pltpu.VMEM((D, D), bf16),
            pltpu.VMEM((1, D), f32),
            pltpu.VMEM((EXPERTS, D), bf16),
            pltpu.VMEM((8, GROUP), jnp.int32),
            pltpu.VMEM((UNITS_DEV, D, 2 * UNIT), bf16),
            pltpu.VMEM((UNITS_DEV, UNIT, D), bf16),
            pltpu.VMEM((N_REQ, TOK, D), bf16),
            pltpu.VMEM((N_REQ, TOK, 1024), bf16),
            pltpu.VMEM((N_REQ, TOK, D), bf16),
            pltpu.VMEM((CHUNKS, ROWS, 128), bf16),
            pltpu.VMEM((N_TP, ROWS, 128), bf16),
            pltpu.VMEM((HALF, ROWS, 256), bf16),
            pltpu.VMEM((CHUNKS, 4, PAGE, 128), bf16),
            pltpu.VMEM((4, 4, PAGE, 128), bf16),
            pltpu.VMEM((N_TP, ROWS, 128), bf16),
            pltpu.VMEM((N_TP, ROWS, 128), bf16),
            pltpu.VMEM((N_TP, ROWS, CW), bf16),
            pltpu.VMEM((N_TP, ROWS, CW), bf16),
            pltpu.VMEM((N_TP, ROWS, CW), bf16),
            pltpu.VMEM((8, ROWS, CW), bf16),
            pltpu.VMEM((N_TP, ROWS, CW), bf16),
            pltpu.VMEM((8, ROWS, CW), bf16),
            pltpu.VMEM((CHUNKS * ROWS, 128), f32),
            pltpu.VMEM((ROWS, CW), f32),
            pltpu.VMEM((8, D), f32),
            pltpu.VMEM((256, 256), bf16),
            pltpu.VMEM((256, 256), bf16),
            pltpu.VMEM((256, 768), bf16),
            pltpu.VMEM((2, 8 * PAGE, 128), bf16),
            pltpu.VMEM((2, 8 * PAGE, 256), bf16),
            pltpu.VMEM((GROUP, D), bf16),
            pltpu.VMEM((GROUP, UNITS_DEV * UNIT), bf16),
            pltpu.VMEM((256, CW), bf16),
            dma((16,)),
            dma((20,)), dma((8,)), dma((8,)),
        ],
        compiler_params=pltpu.CompilerParams(
            collective_id=0, has_side_effects=True, vmem_limit_bytes=63 << 20
        ),
        name="verify_layer",
    )(
        queries, new_kv, residual, placement, lengths, page_table.reshape(2),
        cache_keys, cache_values, parents, accept_leaf, out_weight, norm_gain,
        router_weight.T, expert_ids.T, gate_up, down_weight,
    )
    return pl.pallas_call(
        hand_out,
        out_shape=shapes,
        in_specs=[vmem] * 3,
        out_specs=(vmem, vmem, vmem),
        compiler_params=pltpu.CompilerParams(vmem_limit_bytes=63 << 20),
        name="hand_out",
    )(*(pltpu.with_memory_space_constraint(a, pltpu.VMEM) for a in results))


def solution(mesh):
    in_specs = (
        P(("req", "tp"), None),
        P(("req", "tp"), None),
        P(("req", "tp"), None),
        P("req"),
        P("req"),
        P("req", None, "tp"),
        P(("req", "tp"), None, None),
        P(("req", "tp"), None, None),
        P("req", None),
        P("req"),
        P(),
        P(),
        P(),
        P("req", None),
        P("tp", None, None),
        P("tp", None, None),
    )
    out_specs = (P(("req", "tp"), None), P(("req", "tp"), None), P(("req", "tp"), None))
    return jax.shard_map(
        per_device, mesh=mesh, in_specs=in_specs, out_specs=out_specs, check_vma=False
    )
```

```python
import functools

import jax
import jax.numpy as jnp
from jax import lax
from jax.experimental import pallas as pl
from jax.experimental.pallas import tpu as pltpu
from jax.sharding import PartitionSpec as P

HEADS = 24
KV_HEADS = 8
HEAD = 64
D = 1536
EXPERTS = 40
FF_E = 512
UNIT = 128
UNITS_DEV = 5
DRAFT = 64
PAGE = 128
N_REQ = 8
N_TP = 32
TOK = 4
CHUNKS = 4
CW = D // CHUNKS
HALF = N_TP // 2
ROWS = CHUNKS * TOK
GROUP = N_TP * TOK
FAR = (2, 6, 3, 5, 4)

neg_big = -1e30
norm_eps = 1e-06
MESH = pl.DeviceIdType.MESH
f32 = jnp.float32
bf16 = jnp.bfloat16


def iota(shape, dim):
    return lax.broadcasted_iota(jnp.int32, shape, dim)


def ones_at(mask):
    return jnp.where(mask, 1.0, 0.0).astype(bf16)


def dot(a, b):
    return jnp.dot(a, b, preferred_element_type=f32)


def dot_t(a, b):
    return lax.dot_general(a, b, (((1,), (1,)), ((), ())), preferred_element_type=f32)


def two_heads(block, lo, hi):
    return jnp.concatenate([block * lo, block * hi], axis=0)


def softmax_block(stacked, keys_two, values_two, valid):
    count = keys_two.shape[0] // 2
    scores = dot_t(stacked, keys_two)
    s_lo = jnp.where(valid, scores[:, :count], neg_big)
    s_hi = jnp.where(valid, scores[:, count:], neg_big)
    m_lo = jnp.max(s_lo, axis=1, keepdims=True)
    m_hi = jnp.max(s_hi, axis=1, keepdims=True)
    w_lo = jnp.exp(s_lo - m_lo).astype(bf16)
    w_hi = jnp.exp(s_hi - m_hi).astype(bf16)
    both = dot(jnp.concatenate([w_lo, w_hi], axis=1), values_two)
    out, total = both[:, :128], both[:, 128:]
    first = iota((out.shape[0], 128), 1) < HEAD
    top = jnp.where(first, m_lo, m_hi)
    some = top > 0.5 * neg_big
    return out / total, jnp.where(some, top + jnp.log(total), neg_big)


def two_ones(count):
    row = iota((2 * count, 128), 0)
    lane = iota((2 * count, 128), 1)
    return ones_at((row >= count) == (lane >= HEAD))


def kernel(
    q_hbm, kv_hbm, res_hbm, placement_hbm, lengths_hbm, table_hbm, keys_hbm, vals_hbm,
    par_hbm, leaf_hbm, ow_hbm, gain_hbm, rw_hbm, ids_hbm, gu_hbm, dw_hbm,
    attn_ref, layer_ref, acc_ref,
    placement, lengths, table, kbuf, vbuf,
    par_ref, leaf, ow, gain_ref, rw, ids_ref, gu, dw,
    q8, kv8, res8, qown, qall, kvall, pages_send, pages, osend, orecv, nall, msend, mrow, msum, mnear, mrecv,
    heads_s, chunk_s, flat_s, perm_s, permt_s, lift_s, kz_s, vz_s, nfull, act_s, moe_s,
    wsem, sems, far_sems, row_sems,
):
    g = lax.axis_index("req")
    t = lax.axis_index("tp")
    x = t % 4
    z = t // 4
    row_start = t - x
    half = t // HALF
    t_in = t % HALF

    def req_peer(k):
        return lax.rem(g + 4 + (1 - 2 * ((k - 1) % 2)) * (k // 2), N_REQ)

    def offset(k):
        i, j = (k - 1) // 4, (k - 1) % 4
        along_z = 4 + (1 - 2 * (i % 2)) * ((i + 1) // 2)
        return along_z, 2 + (1 - 2 * (j % 2)) * ((j + 1) // 2)

    def tp_peer(k):
        along_z, along_x = offset(k)
        return lax.rem(z + along_z, 8) * 4 + lax.rem(x + along_x, 4)

    def slot_peer(k):
        return half * HALF + lax.rem(t_in + k, HALF)

    barrier = pltpu.get_barrier_semaphore()

    def greet_req(k, carry):
        pl.semaphore_signal(barrier, inc=1, device_id={"req": req_peer(k)}, device_id_type=MESH)
        return carry

    def greet_tp(k, carry):
        pl.semaphore_signal(barrier, inc=1, device_id={"tp": tp_peer(k)}, device_id_type=MESH)
        return carry

    def load(i, source, target):
        copy = pltpu.make_async_copy(source, target, wsem.at[i])
        copy.start()
        return copy

    lax.fori_loop(1, N_REQ, greet_req, 0)
    lax.fori_loop(1, N_TP, greet_tp, 0)
    load_q = load(0, q_hbm, q8.at[g])
    load_kv = load(1, kv_hbm, kv8.at[g])
    load_res = load(2, res_hbm, res8.at[g])
    load_placement = load(3, placement_hbm, placement)
    load_par = load(4, par_hbm, par_ref)
    load_leaf = load(5, leaf_hbm, leaf)
    load_lengths = load(6, lengths_hbm, lengths)
    load_table = load(7, table_hbm, table)
    load_keys = load(8, keys_hbm, kbuf)
    load_vals = load(9, vals_hbm, vbuf)
    load_gain = load(10, gain_hbm, gain_ref.at[0])
    load_ids = load(11, ids_hbm, ids_ref)
    load_rw = load(12, rw_hbm, rw)
    load_ow = load(13, ow_hbm, ow)
    load_gu = load(14, gu_hbm, gu)
    load_dw = load(15, dw_hbm, dw)

    def page_copy(k, source):
        peer = lax.rem(x + k, 4)
        return pltpu.make_async_remote_copy(
            src_ref=pages_send.at[peer], dst_ref=pages.at[source], send_sem=sems.at[0],
            recv_sem=sems.at[1], device_id={"tp": row_start + peer}, device_id_type=MESH,
        )

    def q8_copy(k, source):
        return pltpu.make_async_remote_copy(
            src_ref=q_hbm, dst_ref=q8.at[source], send_sem=sems.at[2],
            recv_sem=sems.at[3], device_id={"req": req_peer(k)}, device_id_type=MESH,
        )

    def kv8_copy(k, source):
        return pltpu.make_async_remote_copy(
            src_ref=kv_hbm, dst_ref=kv8.at[source], send_sem=sems.at[4],
            recv_sem=sems.at[5], device_id={"req": req_peer(k)}, device_id_type=MESH,
        )

    def res8_copy(k, source):
        return pltpu.make_async_remote_copy(
            src_ref=res_hbm, dst_ref=res8.at[source], send_sem=sems.at[17],
            recv_sem=sems.at[18], device_id={"req": req_peer(k)}, device_id_type=MESH,
        )

    def q_copy(k, source):
        return pltpu.make_async_remote_copy(
            src_ref=qown.at[lax.rem(x + offset(k)[1], 4)], dst_ref=qall.at[source], send_sem=sems.at[6],
            recv_sem=sems.at[19], device_id={"tp": tp_peer(k)}, device_id_type=MESH,
        )

    def kv_copy(k, source):
        return pltpu.make_async_remote_copy(
            src_ref=kvall.at[source], dst_ref=kvall.at[source], send_sem=sems.at[8],
            recv_sem=sems.at[9], device_id={"tp": slot_peer(k)}, device_id_type=MESH,
        )

    def o_copy(k, block, source):
        return pltpu.make_async_remote_copy(
            src_ref=osend.at[block], dst_ref=orecv.at[source], send_sem=sems.at[10],
            recv_sem=sems.at[11], device_id={"tp": tp_peer(k)}, device_id_type=MESH,
        )

    def far_copy(k):
        block = t
        return pltpu.make_async_remote_copy(
            src_ref=nall.at[block], dst_ref=nall.at[block], send_sem=sems.at[12],
            recv_sem=far_sems.at[k], device_id={"tp": lax.rem(z + k, 8) * 4 + x}, device_id_type=MESH,
        )

    def n_copy(block, peer):
        return pltpu.make_async_remote_copy(
            src_ref=nall.at[block], dst_ref=nall.at[block], send_sem=sems.at[12],
            recv_sem=sems.at[13], device_id={"tp": peer}, device_id_type=MESH,
        )

    def row_copy(zone, k):
        peer = lax.rem(x + k, 4)
        return pltpu.make_async_remote_copy(
            src_ref=msend.at[zone * 4 + peer], dst_ref=mrow.at[zone * 4 + x], send_sem=sems.at[14],
            recv_sem=row_sems.at[zone], device_id={"tp": row_start + peer}, device_id_type=MESH,
        )

    def zone_copy(zone):
        return pltpu.make_async_remote_copy(
            src_ref=msum.at[zone], dst_ref=mrecv.at[z], send_sem=sems.at[15],
            recv_sem=sems.at[16], device_id={"tp": zone * 4 + x}, device_id_type=MESH,
        )

    def near_start(k):
        zone = offset(k)[0]
        far = functools.reduce(jnp.logical_or, [zone == f for f in FAR])

        @pl.when(jnp.logical_not(far))
        def _():
            n_copy(t, tp_peer(k)).start()

    def direct_copy(along_z, k):
        peer = lax.rem(z + along_z, 8) * 4 + lax.rem(x + k, 4)
        return pltpu.make_async_remote_copy(
            src_ref=msend.at[peer], dst_ref=mnear.at[t], send_sem=sems.at[14],
            recv_sem=sems.at[7], device_id={"tp": peer}, device_id_type=MESH,
        )

    def await_bytes(refs, index):
        pltpu.make_async_copy(refs, refs, sems.at[index]).wait()

    def each(count, step):
        def body(k, carry):
            step(k)
            return carry

        lax.fori_loop(1, count, body, 0)

    pl.semaphore_wait(barrier, N_REQ - 1 + N_TP - 1)

    each(N_REQ, lambda k: q8_copy(k, g).start())
    each(N_REQ, lambda k: kv8_copy(k, g).start())
    each(N_REQ, lambda k: res8_copy(k, g).start())

    load_table.wait()
    load_keys.wait()
    load_vals.wait()
    for s in range(2):
        page_k = kbuf[table[s]]
        page_v = vbuf[table[s]]
        for c in range(CHUNKS):
            pages_send[c, s] = page_k[:, c * 128:(c + 1) * 128]
            pages_send[c, 2 + s] = page_v[:, c * 128:(c + 1) * 128]
    each(4, lambda k: page_copy(k, x).start())
    pages[x] = pages_send[x]
    lane_one = iota((1, 128), 1)
    lo = ones_at(lane_one < HEAD)
    hi = ones_at(lane_one >= HEAD)

    load_q.wait()
    load_placement.wait()
    source_group = lax.shift_right_logical(placement[half], 1)
    heads_s[...] = jnp.zeros_like(heads_s)
    await_bytes(q8.at[0:N_REQ - 1], 3)
    q_in = q8[source_group].astype(f32) * (HEAD ** -0.5)
    for c in range(CHUNKS):
        for r in range(3):
            for k in range(2):
                at = c * CW + (k * 3 + r) * HEAD
                row = c * ROWS + r * TOK
                heads_s[row:row + TOK, k * HEAD:(k + 1) * HEAD] = q_in[:, at:at + HEAD]
    own_q = heads_s[...].astype(bf16).reshape(CHUNKS, ROWS, 128)
    qown[...] = own_q
    qall[t] = qown[x]
    each(N_TP, lambda k: q_copy(k, t).start())
    load_kv.wait()
    await_bytes(kv8.at[0:N_REQ - 1], 5)
    kv_in = kv8[source_group].astype(f32)
    for c in range(CHUNKS):
        chunk_s[c * TOK:(c + 1) * TOK, 0:128] = kv_in[:, c * 128:(c + 1) * 128]
        chunk_s[c * TOK:(c + 1) * TOK, 128:256] = kv_in[:, 512 + c * 128:512 + (c + 1) * 128]
    kvall[t_in] = chunk_s[:, 0:256].astype(bf16)
    each(HALF, lambda k: kv_copy(k, t_in).start())
    load_res.wait()
    await_bytes(res8.at[0:N_REQ - 1], 18)
    own_res = res8[source_group].astype(f32)

    row_a = iota((256, 256), 0)
    row_b = iota((256, 256), 1)
    perm_s[...] = ones_at(
        row_b == ((row_a & 63) >> 2) * ROWS + (row_a >> 6) * TOK + (row_a & 3)
    )
    permt_s[...] = ones_at(
        row_a == ((row_b & 63) >> 2) * ROWS + (row_b >> 6) * TOK + (row_b & 3)
    )

    lift_r = iota((256, 768), 0)
    lift_c = iota((256, 768), 1)
    lift_s[...] = ones_at(
        ((lift_r >> 4) == ((lift_c & 255) >> 4)) & ((lift_r & 15) == 3 * TOK + (lift_c >> 8))
    )
    span = 4 * PAGE
    ones_page = two_ones(span)
    block_row = iota((256, 128), 0) & (ROWS - 1)
    block_lane = iota((256, 128), 1)
    diag = (block_lane & (HEAD - 1)) == block_row
    load_lengths.wait()
    await_bytes(pages.at[0:3], 1)
    for s in range(2):
        kz_s[s] = two_heads(pages[:, s].reshape(span, 128), lo, hi)
        vz_s[s, :, 0:128] = two_heads(pages[:, 2 + s].reshape(span, 128), lo, hi)
        vz_s[s, :, 128:256] = ones_page
    await_bytes(qall.at[0:N_TP - 1], 19)
    for s in range(2):
        valid = row_start * PAGE + iota((1, span), 1) < lengths[s]
        out, lse = softmax_block(
            qall[s * HALF:(s + 1) * HALF].reshape(256, 128), kz_s[s], vz_s[s], valid
        )
        first = lse.astype(bf16).astype(f32)
        rest = lse - first
        second = rest.astype(bf16).astype(f32)
        parts = [jnp.where(diag, part, 0.0).astype(bf16) for part in (first, second, rest - second)]
        lifted = dot(lift_s[...], jnp.concatenate(parts, axis=0))
        osend[s * HALF:(s + 1) * HALF] = (
            jnp.where(block_row < 3 * TOK, out, lifted).astype(bf16).reshape(HALF, ROWS, 128)
        )

    each(N_TP, lambda k: o_copy(k, tp_peer(k), t).start())
    orecv[t] = osend[t]

    node_m = iota((DRAFT, DRAFT), 0)
    node_n = iota((DRAFT, DRAFT), 1)
    load_par.wait()
    load_leaf.wait()
    parent_row = par_ref[pl.ds(half, 1), :]
    reach_t = ones_at(((node_m == parent_row) & (node_n > 0)) | (node_m == node_n))
    for _ in range(6):
        reach_t = jnp.minimum(dot(reach_t, reach_t), 1.0).astype(bf16)
    own_node = t_in * TOK + (iota((ROWS, DRAFT), 0) & 3)
    lane_node = iota((ROWS, DRAFT), 1)
    tree_node = t_in * TOK + (iota((CHUNKS * ROWS, DRAFT), 0) & 3)
    tree_lane = iota((CHUNKS * ROWS, DRAFT), 1)
    spread_row = iota((DRAFT, 256), 0)
    spread_lane = iota((DRAFT, 256), 1)
    spread = ones_at(spread_row == (spread_lane >> 4) * TOK + (spread_lane & 3))
    same_chunk = ((iota((ROWS, 256), 1) >> 2) & 3) == (iota((ROWS, 256), 0) >> 2)
    tree_chunk = ((iota((CHUNKS * ROWS, 256), 1) >> 2) & 3) == (iota((CHUNKS * ROWS, 256), 0) >> 4)
    own_reach = dot_t(ones_at(tree_lane == tree_node), reach_t).astype(bf16)
    tree_valid = jnp.where(tree_chunk, dot(own_reach, spread), 0.0) > 0.5
    flags = dot_t(ones_at(lane_node == leaf[half]), reach_t)
    rank = dot(flags.astype(bf16), ones_at(node_m <= node_n)) - 1.0
    chosen = ones_at((flags > 0.5) & (rank == own_node.astype(f32)))
    choice = jnp.where(same_chunk, dot(chosen, spread), 0.0).astype(bf16)
    await_bytes(kvall.at[0:HALF - 1], 9)
    kv_slot = kvall[...].reshape(256, 256)
    accepted = dot(choice, kv_slot)
    for c in range(CHUNKS):
        acc_ref[:, c * 128:(c + 1) * 128] = accepted[c * TOK:(c + 1) * TOK, 0:128].astype(bf16)
        acc_ref[:, 512 + c * 128:512 + (c + 1) * 128] = (
            accepted[c * TOK:(c + 1) * TOK, 128:256].astype(bf16)
        )
    tree_out, tree_lse = softmax_block(
        own_q.reshape(CHUNKS * ROWS, 128), two_heads(kv_slot[:, 0:128], lo, hi),
        jnp.concatenate([two_heads(kv_slot[:, 128:256], lo, hi), two_ones(256)], axis=1), tree_valid,
    )
    drop = ones_at(
        ((row_a >> 4) == (row_b >> 4)) & ((row_b & 15) >= 3 * TOK) & ((row_b & 15) < 3 * TOK + 3)
    )

    await_bytes(orecv.at[0:N_TP - 1], 11)
    lse_parts = []
    for s in range(2):
        packed = orecv[s * HALF:(s + 1) * HALF].reshape(256, 128)
        own_lane = jnp.where(diag, dot(drop, packed), 0.0)
        lse_lo = jnp.sum(jnp.where(block_lane < HEAD, own_lane, 0.0), axis=1, keepdims=True)
        lse_hi = jnp.sum(jnp.where(block_lane < HEAD, 0.0, own_lane), axis=1, keepdims=True)
        lse_parts.append(jnp.where(block_lane < HEAD, lse_lo, lse_hi))
    lse_all = jnp.concatenate(lse_parts, axis=0).reshape(N_TP // 4, CHUNKS * ROWS, 128)
    out_all = orecv[...].reshape(N_TP // 4, CHUNKS * ROWS, 128).astype(f32)
    top = jnp.maximum(jnp.max(lse_all, axis=0), tree_lse)
    scale = jnp.exp(lse_all - top[None])
    tree_scale = jnp.exp(tree_lse - top)
    total = jnp.sum(scale, axis=0) + tree_scale
    joined = (jnp.sum(scale * out_all, axis=0) + tree_scale * tree_out) / total
    for c in range(CHUNKS):
        for r in range(3):
            for k in range(2):
                at = c * CW + (k * 3 + r) * HEAD
                row = c * ROWS + r * TOK
                flat_s[0:TOK, at:at + HEAD] = joined[row:row + TOK, k * HEAD:(k + 1) * HEAD]
    attn = flat_s[0:TOK, :].astype(bf16)
    attn_ref[...] = attn

    load_ow.wait()
    load_gain.wait()
    hidden = own_res + dot(attn, ow[...])
    mean = jnp.mean(hidden * hidden, axis=-1, keepdims=True)
    normed = (hidden * lax.rsqrt(mean + norm_eps) * gain_ref[...]).astype(bf16).astype(f32)
    for c in range(CHUNKS):
        chunk_s[c * TOK:(c + 1) * TOK, :] = normed[:, c * CW:(c + 1) * CW]
    nall[t] = chunk_s[...].astype(bf16)

    for k in FAR:
        far_copy(k).start()
    each(N_TP, lambda k: near_start(k))
    expert_row = iota((EXPERTS, GROUP), 0)
    load_ids.wait()
    ids = ids_ref[...]
    picked = expert_row == ids[0:1]
    for k in range(1, ids.shape[0]):
        picked = picked | (expert_row == ids[k:k + 1])
    for k in FAR:
        far_copy(k).wait_recv()
        block = lax.rem(z + 8 - k, 8) * 4 + x
        for i in range(1, 4):
            n_copy(block, row_start + lax.rem(x + i, 4)).start()
    load_rw.wait()
    load_gu.wait()
    load_dw.wait()
    await_bytes(nall.at[0:N_TP - 1 - len(FAR)], 13)
    for s in range(2):
        rows = dot(perm_s[...], nall[s * HALF:(s + 1) * HALF].reshape(256, CW)).astype(bf16)
        for c in range(CHUNKS):
            nfull[s * DRAFT:(s + 1) * DRAFT, c * CW:(c + 1) * CW] = rows[c * DRAFT:(c + 1) * DRAFT]
    normed_all = nfull[...]
    expo = jnp.where(picked, jnp.exp(dot_t(rw[...], normed_all)), 0.0)
    routing = expo / jnp.sum(expo, axis=0, keepdims=True)
    first_expert = t * UNITS_DEV // (FF_E // UNIT)
    two = jnp.concatenate(
        [
            jnp.sum(jnp.where(expert_row == first_expert + k, routing, 0.0), axis=0, keepdims=True)
            for k in range(2)
        ]
        + [jnp.zeros((GROUP - 2, GROUP), f32)],
        axis=0,
    )
    columns = jnp.transpose(two)
    for u in range(UNITS_DEV):
        same = (t * UNITS_DEV + u) // (FF_E // UNIT) == first_expert
        share = jnp.where(same, columns[:, 0:1], columns[:, 1:2])
        both = dot(normed_all, gu[u])
        gate = both[:, :UNIT]
        active = gate / (1.0 + jnp.exp(-gate)) * both[:, UNIT:] * share
        act_s[:, u * UNIT:(u + 1) * UNIT] = active.astype(bf16)
    moe = dot(act_s[...], dw[...].reshape(UNITS_DEV * UNIT, D)).astype(bf16)
    for s in range(2):
        for c in range(CHUNKS):
            moe_s[c * DRAFT:(c + 1) * DRAFT, :] = moe[s * DRAFT:(s + 1) * DRAFT, c * CW:(c + 1) * CW]
        msend[s * HALF:(s + 1) * HALF] = (
            dot(permt_s[...], moe_s[...]).astype(bf16).reshape(HALF, ROWS, CW)
        )

    zones = [lax.rem(z + k, 8) for k in (4, 3, 5)]
    for zone in zones:
        for k in (2, 1, 3):
            row_copy(zone, k).start()
    for along_z in (2, 6, 1, 7):
        for k in (2, 1, 3, 0):
            direct_copy(along_z, k).start()
    for k in (2, 1, 3):
        direct_copy(0, k).start()
    await_bytes(pages_send.at[0:3], 0)
    await_bytes(q8.at[0:N_REQ - 1], 2)
    await_bytes(kv8.at[0:N_REQ - 1], 4)
    await_bytes(res8.at[0:N_REQ - 1], 17)
    await_bytes(qall.at[0:N_TP - 1], 6)
    await_bytes(kvall.at[0:HALF - 1], 8)
    await_bytes(osend.at[0:N_TP - 1], 10)
    await_bytes(nall.at[0:N_TP - 1], 12)
    for i, zone in enumerate(zones):
        pltpu.make_async_copy(mrow.at[0:3], mrow.at[0:3], row_sems.at[zone]).wait()
        part = msend[zone * 4 + x].astype(f32)
        for k in range(1, 4):
            part = part + mrow[zone * 4 + lax.rem(x + k, 4)].astype(f32)
        msum[zone] = part.astype(bf16)
        zone_copy(zone).start()
    moe_own = msend[t].astype(f32)
    await_bytes(mnear.at[0:19], 7)
    for along_z in (2, 6, 1, 7):
        for k in range(4):
            moe_own = moe_own + mnear[lax.rem(z + along_z, 8) * 4 + lax.rem(x + k, 4)].astype(f32)
    for k in range(1, 4):
        moe_own = moe_own + mnear[z * 4 + lax.rem(x + k, 4)].astype(f32)
    await_bytes(mrecv.at[0:3], 16)
    for zone in zones:
        moe_own = moe_own + mrecv[zone].astype(f32)
    for c in range(CHUNKS):
        flat_s[0:TOK, c * CW:(c + 1) * CW] = moe_own[c * TOK:(c + 1) * TOK, :]
    layer_ref[...] = (hidden + flat_s[0:TOK, :]).astype(bf16)
    await_bytes(msend.at[0:28], 14)
    await_bytes(msum.at[0:3], 15)


def hand_out(attn_in, layer_in, acc_in, attn_out, layer_out, acc_out):
    attn_out[...] = attn_in[...]
    layer_out[...] = layer_in[...]
    acc_out[...] = acc_in[...]


def per_device(
    queries, new_kv, residual, placement, lengths, page_table, cache_keys, cache_values,
    parents, accept_leaf, out_weight, norm_gain, router_weight, expert_ids, gate_up, down_weight,
):
    vmem = pl.BlockSpec(memory_space=pltpu.VMEM)
    hbm = pl.BlockSpec(memory_space=pltpu.MemorySpace.HBM)
    dma = pltpu.SemaphoreType.DMA
    shapes = (
        jax.ShapeDtypeStruct((TOK, D), bf16),
        jax.ShapeDtypeStruct((TOK, D), bf16),
        jax.ShapeDtypeStruct((TOK, 1024), bf16),
    )
    results = pl.pallas_call(
        kernel,
        out_shape=tuple(pltpu.VMEM(a.shape, a.dtype) for a in shapes),
        in_specs=[hbm] * 16,
        out_specs=(vmem, vmem, vmem),
        scratch_shapes=[
            pltpu.SMEM((2,), jnp.int32),
            pltpu.SMEM((2,), jnp.int32),
            pltpu.SMEM((2,), jnp.int32),
            pltpu.VMEM((2, PAGE, 512), bf16),
            pltpu.VMEM((2, PAGE, 512), bf16),
            pltpu.VMEM((2, DRAFT), jnp.int32),
            pltpu.SMEM((2,), jnp.int32),
            pltpu.VMEM((D, D), bf16),
            pltpu.VMEM((1, D), f32),
            pltpu.VMEM((EXPERTS, D), bf16),
            pltpu.VMEM((8, GROUP), jnp.int32),
            pltpu.VMEM((UNITS_DEV, D, 2 * UNIT), bf16),
            pltpu.VMEM((UNITS_DEV, UNIT, D), bf16),
            pltpu.VMEM((N_REQ, TOK, D), bf16),
            pltpu.VMEM((N_REQ, TOK, 1024), bf16),
            pltpu.VMEM((N_REQ, TOK, D), bf16),
            pltpu.VMEM((CHUNKS, ROWS, 128), bf16),
            pltpu.VMEM((N_TP, ROWS, 128), bf16),
            pltpu.VMEM((HALF, ROWS, 256), bf16),
            pltpu.VMEM((CHUNKS, 4, PAGE, 128), bf16),
            pltpu.VMEM((4, 4, PAGE, 128), bf16),
            pltpu.VMEM((N_TP, ROWS, 128), bf16),
            pltpu.VMEM((N_TP, ROWS, 128), bf16),
            pltpu.VMEM((N_TP, ROWS, CW), bf16),
            pltpu.VMEM((N_TP, ROWS, CW), bf16),
            pltpu.VMEM((N_TP, ROWS, CW), bf16),
            pltpu.VMEM((8, ROWS, CW), bf16),
            pltpu.VMEM((N_TP, ROWS, CW), bf16),
            pltpu.VMEM((8, ROWS, CW), bf16),
            pltpu.VMEM((CHUNKS * ROWS, 128), f32),
            pltpu.VMEM((ROWS, CW), f32),
            pltpu.VMEM((8, D), f32),
            pltpu.VMEM((256, 256), bf16),
            pltpu.VMEM((256, 256), bf16),
            pltpu.VMEM((256, 768), bf16),
            pltpu.VMEM((2, 8 * PAGE, 128), bf16),
            pltpu.VMEM((2, 8 * PAGE, 256), bf16),
            pltpu.VMEM((GROUP, D), bf16),
            pltpu.VMEM((GROUP, UNITS_DEV * UNIT), bf16),
            pltpu.VMEM((256, CW), bf16),
            dma((16,)),
            dma((20,)), dma((8,)), dma((8,)),
        ],
        compiler_params=pltpu.CompilerParams(
            collective_id=0, has_side_effects=True, vmem_limit_bytes=63 << 20
        ),
        name="verify_layer",
    )(
        queries, new_kv, residual, placement, lengths, page_table.reshape(2),
        cache_keys, cache_values, parents, accept_leaf, out_weight, norm_gain,
        router_weight.T, expert_ids.T, gate_up, down_weight,
    )
    return pl.pallas_call(
        hand_out,
        out_shape=shapes,
        in_specs=[vmem] * 3,
        out_specs=(vmem, vmem, vmem),
        compiler_params=pltpu.CompilerParams(vmem_limit_bytes=63 << 20),
        name="hand_out",
    )(*(pltpu.with_memory_space_constraint(a, pltpu.VMEM) for a in results))


def solution(mesh):
    in_specs = (
        P(("req", "tp"), None),
        P(("req", "tp"), None),
        P(("req", "tp"), None),
        P("req"),
        P("req"),
        P("req", None, "tp"),
        P(("req", "tp"), None, None),
        P(("req", "tp"), None, None),
        P("req", None),
        P("req"),
        P(),
        P(),
        P(),
        P("req", None),
        P("tp", None, None),
        P("tp", None, None),
    )
    out_specs = (P(("req", "tp"), None), P(("req", "tp"), None), P(("req", "tp"), None))
    return jax.shard_map(
        per_device, mesh=mesh, in_specs=in_specs, out_specs=out_specs, check_vma=False
    )
```
